32 devices in a mesh: ctx: 8 (over z, core), fsdp: 4 (over y, x).
Axes of the slice: x: 2, y: 2, z: 4, core: 2. Of those that a mesh axis runs over, the one named last changes fastest.
Arguments:
- hidden_in: bfloat16 [4, 1024, 1024], P('fsdp', 'ctx'), may hold values from -6 to 6
- positions: int32 [4, 1024], P('fsdp', 'ctx'), may hold values from 0 to 1023, as said below
- attn_gain: bfloat16 [1024], P(('ctx', 'fsdp')), may hold values from 0.5 to 1.5
- w_query: bfloat16 [1024, 1024], P(('ctx', 'fsdp'))
- w_key: bfloat16 [1024, 128], P(('ctx', 'fsdp'))
- w_value: bfloat16 [1024, 128], P(('ctx', 'fsdp')), may hold values from -0.1875 to 0.1875
- w_out: bfloat16 [1024, 1024], P(('ctx', 'fsdp')), may hold values from -4 to 4
- ffn_gain: bfloat16 [1024], P(('ctx', 'fsdp')), may hold values from 0.5 to 1.5
- w_gate: bfloat16 [1024, 2816], P(('ctx', 'fsdp')), may hold values from -0.1875 to 0.1875
- w_up: bfloat16 [1024, 2816], P(('ctx', 'fsdp')), may hold values from -0.1875 to 0.1875
- w_down: bfloat16 [2816, 1024], P(('ctx', 'fsdp')), may hold values from -0.109375 to 0.109375
- cotangent: bfloat16 [4, 1024, 1024], P('fsdp', 'ctx'), may hold values from -6 to 6
Outputs:
- block_out: float32 [4, 1024, 1024], P('fsdp', 'ctx')
- input_grad: float32 [4, 1024, 1024], P('fsdp', 'ctx')
- attn_gain_grad: float32 [1024], P(('ctx', 'fsdp'))
- w_query_grad: float32 [1024, 1024], P(('ctx', 'fsdp'))
- w_key_grad: float32 [1024, 128], P(('ctx', 'fsdp'))
- w_value_grad: float32 [1024, 128], P(('ctx', 'fsdp'))
- w_out_grad: float32 [1024, 1024], P(('ctx', 'fsdp'))
- ffn_gain_grad: float32 [1024], P(('ctx', 'fsdp'))
- w_gate_grad: float32 [1024, 2816], P(('ctx', 'fsdp'))
- w_up_grad: float32 [1024, 2816], P(('ctx', 'fsdp'))
- w_down_grad: float32 [2816, 1024], P(('ctx', 'fsdp'))
The draws below stay inside these ranges and needn't reach their ends.
Inputs may be any that keep to these rules, and one draw needn't show every extreme that they name: In each sequence the 128 tokens stored at one index of ctx are the positions of two blocks of 64 consecutive positions, block b and then block 2 n - 1 - b, n being the number of indices of ctx, each in ascending order; every position of the sequence occurs once.
All inputs are finite; a program needn't handle non-finite values.
Results may differ from the reference program's by a relative error of at most 0.023.
The reference program's roundings to bfloat16 on the way count: a program that leaves them out, or rounds other values in their place, can miss the bound.
Values may be sent and summed in bfloat16 or wider, within the bound.
No kernel may reach another device: no remote copies, remote signals or barrier semaphores. Data moves between devices by JAX's collectives and lax.ppermute only.
A program may use at most 128 MiB of HBM per device.

```python
import jax
import jax.numpy as jnp
from jax import lax

D = 1024
HEADS = 16
KV_HEADS = 2
HEAD_DIM = 64
FF = 2816
BLK = 64
KVD = 128
TOK_DEV = 128
SEQ_LEN = 1024
SEQS = 4


def query_base(key):
    return jax.random.normal(jax.random.fold_in(key, 101), (D, D), jnp.float32) * D ** (-0.5)


def draw_w_query(key, part):
    return query_base(key).astype(jnp.bfloat16)


def draw_w_key(key, part):
    own = jax.random.normal(jax.random.fold_in(key, 202), (D, KV_HEADS * HEAD_DIM), jnp.float32) * D ** (-0.5)
    return own.astype(jnp.bfloat16)


def draw_positions(key, part):
    blocks = SEQ_LEN // TOK_DEV
    seq_keys = jax.random.split(jax.random.fold_in(key, 303), SEQS)
    block_order = jax.vmap(lambda one_key: jax.random.permutation(one_key, blocks))(seq_keys).astype(jnp.int32)
    offsets = jnp.arange(BLK, dtype=jnp.int32)
    first_half = block_order[:, :, None] * BLK + offsets[None, None, :]
    second_half = (2 * blocks - 1 - block_order)[:, :, None] * BLK + offsets[None, None, :]
    return jnp.concatenate([first_half, second_half], axis=2).reshape(SEQS, SEQ_LEN).astype(jnp.int32)


def level_of(stream_key, extent, cuts, least, top_value):
    loudness, own = 1.0, jax.random.fold_in(stream_key, 6)
    for dim, blocks in cuts:
        steps = jnp.exp(jax.random.uniform(jax.random.fold_in(own, dim), (blocks,), jnp.float32, least / len(cuts), top_value / len(cuts)))
        loudness = loudness * jnp.repeat(steps, extent[dim] // blocks).reshape([-1 if axis == dim else 1 for axis in range(len(extent))])
    return loudness


def gaussian(own_key, extent, deviation, reach, cuts=(), kind=jnp.bfloat16):
    array = deviation * jax.random.normal(own_key, extent, jnp.float32)
    if cuts:
        array = array * level_of(own_key, extent, cuts, -0.22, 0.18)
    return jnp.clip(array, -reach, reach).astype(kind)


def setup_inputs(seed: int = 0) -> dict:
    key_of = jax.random.split(jax.random.key(seed), 13)
    hidden_in = gaussian(key_of[0], (SEQS, SEQ_LEN, D), 1.0, 6.0, ((0, 4), (1, 8)))
    positions = draw_positions(jax.random.fold_in(key_of[12], 71), 0)
    attn_gain = jnp.clip(1.0 + 0.1 * jax.random.normal(key_of[2], (D,), jnp.float32), 0.5, 1.5).astype(jnp.bfloat16)
    w_query = draw_w_query(jax.random.fold_in(key_of[12], 71), 0)
    w_key = draw_w_key(jax.random.fold_in(key_of[12], 71), 0)
    w_value = gaussian(key_of[5], (D, KVD), D ** -0.5, 0.1875, ((0, 32),))
    w_out = gaussian(key_of[6], (D, D), (max(2 * D // SEQ_LEN, 1)) ** -0.5, 4.0, ((0, 32),))
    ffn_gain = jnp.clip(1.0 + 0.1 * jax.random.normal(key_of[7], (D,), jnp.float32), 0.5, 1.5).astype(jnp.bfloat16)
    w_gate = gaussian(key_of[8], (D, FF), D ** -0.5, 0.1875, ((0, 32),))
    w_up = gaussian(key_of[9], (D, FF), D ** -0.5, 0.1875, ((0, 32),))
    w_down = gaussian(key_of[10], (FF, D), FF ** -0.5, 0.109375, ((0, 32),))
    cotangent = gaussian(key_of[11], (SEQS, SEQ_LEN, D), 1.0, 6.0, ((0, 4), (1, 8)))
    return dict(hidden_in=hidden_in, positions=positions, attn_gain=attn_gain, w_query=w_query, w_key=w_key, w_value=w_value, w_out=w_out, ffn_gain=ffn_gain, w_gate=w_gate, w_up=w_up, w_down=w_down, cotangent=cotangent)


epsilon = 1e-05
rope_base = 10000.0
masked_score = -1e+30

def dot32(left, right):
    return jnp.dot(left, right, preferred_element_type=jnp.float32)

def rounded(values):
    return lax.optimization_barrier(values.astype(jnp.bfloat16)).astype(jnp.float32)

def rope_tables(position):
    half_dim = HEAD_DIM // 2
    steps_f = jnp.arange(half_dim, dtype=jnp.float32)
    frequency = jnp.exp(steps_f * (-2.0 * jnp.log(jnp.float32(rope_base)) / HEAD_DIM))
    angles = position.astype(jnp.float32)[:, None] * frequency[None, :]
    cosine = jnp.concatenate([jnp.cos(angles), jnp.cos(angles)], axis=1)
    sine = jnp.concatenate([jnp.sin(angles), jnp.sin(angles)], axis=1)
    return (cosine, sine)

def rotate(values, cosine, sine):
    half_dim = values.shape[-1] // 2
    turned = jnp.concatenate([-values[..., half_dim:], values[..., :half_dim]], axis=-1)
    return values * cosine[:, None, :] + turned * sine[:, None, :]

def rotate_back(grad_in, cosine, sine):
    half_dim = grad_in.shape[-1] // 2
    shifted = grad_in * sine[:, None, :]
    turned = jnp.concatenate([shifted[..., half_dim:], -shifted[..., :half_dim]], axis=-1)
    return grad_in * cosine[:, None, :] + turned

def normalize(values, gain):
    norm_scale = lax.rsqrt(lax.optimization_barrier(jnp.mean(values * values, axis=-1, keepdims=True)) + epsilon)
    plain = values * norm_scale
    return (plain, norm_scale, plain * gain.astype(jnp.float32)[None, :])

def norm_back(d_out, plain, norm_scale, gain):
    gain_grad = lax.optimization_barrier(jnp.sum(d_out * plain, axis=0))
    scaled = d_out * gain.astype(jnp.float32)[None, :]
    d_in = norm_scale * (scaled - plain * lax.optimization_barrier(jnp.mean(scaled * plain, axis=-1, keepdims=True)))
    return (d_in, gain_grad)

def attend(queries, keys_all, values_all, position):
    group = HEADS // KV_HEADS
    length = queries.shape[0]
    q_rows = min(512, length)
    count = length // q_rows
    factor = HEAD_DIM ** (-0.5)
    keys_f = keys_all.astype(jnp.float32)
    values_f = values_all.astype(jnp.float32)

    def one_block(pieces):
        q_block, q_pos = pieces
        scores = jnp.einsum('qkgd,lkd->kgql', q_block.astype(jnp.float32), keys_f) * factor
        allowed = position[None, None, None, :] <= q_pos[None, None, :, None]
        scores = jnp.where(allowed, scores, masked_score)
        highest = lax.optimization_barrier(jnp.max(scores, axis=-1, keepdims=True))
        summed = lax.optimization_barrier(jnp.sum(jnp.where(allowed, jnp.exp(scores - highest), 0.0), axis=-1, keepdims=True))
        log_total = highest + jnp.log(summed)
        probs = jnp.where(allowed, jnp.exp(scores - log_total), 0.0)
        outputs = jnp.einsum('kgql,lkd->qkgd', rounded(probs), values_f)
        return (outputs.astype(jnp.bfloat16), log_total[..., 0])
    outs_blocks, lse_blocks = lax.map(one_block, (queries.reshape(count, q_rows, KV_HEADS, group, HEAD_DIM), position.reshape(count, q_rows)))
    return (outs_blocks.reshape(length, KV_HEADS, group, HEAD_DIM), lse_blocks)

def attend_back(queries, keys_all, values_all, position, outputs, d_out, lse_blocks):
    group = HEADS // KV_HEADS
    length = queries.shape[0]
    q_rows = min(512, length)
    count = length // q_rows
    factor = HEAD_DIM ** (-0.5)
    keys_f = keys_all.astype(jnp.float32)
    values_f = values_all.astype(jnp.float32)

    def one_block(state, pieces):
        key_grad, value_grad = state
        q_block, q_pos, o_block, do_block, lse_block = pieces
        q_f = q_block.astype(jnp.float32)
        do_f = do_block.astype(jnp.float32)
        delta = jnp.einsum('qkgd,qkgd->kgq', do_f, o_block.astype(jnp.float32))
        scores = jnp.einsum('qkgd,lkd->kgql', q_f, keys_f) * factor
        allowed = position[None, None, None, :] <= q_pos[None, None, :, None]
        scores = jnp.where(allowed, scores, masked_score)
        probs = jnp.where(allowed, jnp.exp(scores - lse_block[..., None]), 0.0)
        value_grad = value_grad + jnp.einsum('kgql,qkgd->lkd', rounded(probs), do_f)
        d_probs = jnp.einsum('qkgd,lkd->kgql', do_f, values_f)
        d_scores = rounded(probs * (d_probs - delta[..., None]) * factor)
        q_grad = jnp.einsum('kgql,lkd->qkgd', d_scores, keys_f)
        key_grad = key_grad + jnp.einsum('kgql,qkgd->lkd', d_scores, q_f)
        return ((key_grad, value_grad), q_grad)
    zeros_kv = jnp.zeros((length, KV_HEADS, HEAD_DIM), jnp.float32)
    shape_q = (count, q_rows, KV_HEADS, group, HEAD_DIM)
    (key_grad, value_grad), q_grads = lax.scan(one_block, (zeros_kv, zeros_kv), (queries.reshape(shape_q), position.reshape(count, q_rows), outputs.reshape(shape_q), d_out.reshape(shape_q), lse_blocks))
    return (q_grads.reshape(length, KV_HEADS, group, HEAD_DIM), key_grad, value_grad)

def one_sequence(weights, pieces):
    attn_gain, w_query, w_key, w_value, w_out, ffn_gain, w_gate, w_up, w_down = weights
    hidden_in, position, cotangent = pieces
    length = hidden_in.shape[0]
    group = HEADS // KV_HEADS
    resid_in = hidden_in.astype(jnp.float32)
    plain_a, scale_a, normed_a = normalize(resid_in, attn_gain)
    normed_b = normed_a.astype(jnp.bfloat16)
    cosine, sine = rope_tables(position)
    queries = rotate(dot32(normed_b, w_query).reshape(length, HEADS, HEAD_DIM), cosine, sine).astype(jnp.bfloat16)
    keys_all = rotate(dot32(normed_b, w_key).reshape(length, KV_HEADS, HEAD_DIM), cosine, sine).astype(jnp.bfloat16)
    values_all = dot32(normed_b, w_value).astype(jnp.bfloat16).reshape(length, KV_HEADS, HEAD_DIM)
    queries = queries.reshape(length, KV_HEADS, group, HEAD_DIM)
    attn_heads, lse_blocks = attend(queries, keys_all, values_all, position)
    attn_flat = attn_heads.reshape(length, D)
    resid_mid = resid_in + dot32(attn_flat, w_out)
    plain_f, scale_f, normed_f = normalize(resid_mid, ffn_gain)
    normed_h = normed_f.astype(jnp.bfloat16)
    gate_proj = dot32(normed_h, w_gate)
    up_proj = dot32(normed_h, w_up)
    activation = (jax.nn.silu(gate_proj) * up_proj).astype(jnp.bfloat16)
    block_out = resid_mid + dot32(activation, w_down)
    w_down_grad = dot32(activation.T, cotangent)
    act_grad = dot32(cotangent, w_down.T)
    sigmoid_g = jax.nn.sigmoid(gate_proj)
    silu_g = gate_proj * sigmoid_g
    up_grad_b = (act_grad * silu_g).astype(jnp.bfloat16)
    gate_grad_b = (act_grad * up_proj * sigmoid_g * (1.0 + gate_proj * (1.0 - sigmoid_g))).astype(jnp.bfloat16)
    w_gate_grad = dot32(normed_h.T, gate_grad_b)
    w_up_grad = dot32(normed_h.T, up_grad_b)
    normed_grad = dot32(gate_grad_b, w_gate.T) + dot32(up_grad_b, w_up.T)
    mid_norm_grad, ffn_gain_grad = norm_back(normed_grad, plain_f, scale_f, ffn_gain)
    mid_grad = cotangent.astype(jnp.float32) + mid_norm_grad
    mid_grad_b = mid_grad.astype(jnp.bfloat16)
    w_out_grad = dot32(attn_flat.T, mid_grad_b)
    attn_grad = dot32(mid_grad_b, w_out.T).astype(jnp.bfloat16).reshape(length, KV_HEADS, group, HEAD_DIM)
    query_grad, key_grad, value_grad = attend_back(queries, keys_all, values_all, position, attn_heads, attn_grad, lse_blocks)
    query_grad_b = rotate_back(query_grad.reshape(length, HEADS, HEAD_DIM), cosine, sine).astype(jnp.bfloat16).reshape(length, D)
    key_grad_b = rotate_back(key_grad, cosine, sine).astype(jnp.bfloat16).reshape(length, KV_HEADS * HEAD_DIM)
    value_grad_b = value_grad.astype(jnp.bfloat16).reshape(length, KV_HEADS * HEAD_DIM)
    w_query_grad = dot32(normed_b.T, query_grad_b)
    w_key_grad = dot32(normed_b.T, key_grad_b)
    w_value_grad = dot32(normed_b.T, value_grad_b)
    input_norm_grad = dot32(query_grad_b, w_query.T) + dot32(key_grad_b, w_key.T) + dot32(value_grad_b, w_value.T)
    in_norm_grad, attn_gain_grad = norm_back(input_norm_grad, plain_a, scale_a, attn_gain)
    input_grad = mid_grad + in_norm_grad
    return ((block_out, input_grad), (attn_gain_grad, w_query_grad, w_key_grad, w_value_grad, w_out_grad, ffn_gain_grad, w_gate_grad, w_up_grad, w_down_grad))

def reference(hidden_in, positions, attn_gain, w_query, w_key, w_value, w_out, ffn_gain, w_gate, w_up, w_down, cotangent):
    weights = (attn_gain, w_query, w_key, w_value, w_out, ffn_gain, w_gate, w_up, w_down)

    def step_fn(totals, pieces):
        results, partial_grads = one_sequence(weights, pieces)
        return (tuple((total + part for total, part in zip(totals, partial_grads))), results)
    zero_grads = tuple((jnp.zeros(weight.shape, jnp.float32) for weight in weights))
    gradients, results = lax.scan(step_fn, zero_grads, (hidden_in, positions, cotangent))
    return (results[0], results[1], gradients[0], gradients[1], gradients[2], gradients[3], gradients[4], gradients[5], gradients[6], gradients[7], gradients[8])
```

```python
import jax
import jax.numpy as jnp
from jax import lax
from jax.sharding import PartitionSpec as P

HEAD_DIM = 64

epsilon = 1e-05
rope_base = 10000.0
masked_score = -1e30
bf16 = jnp.bfloat16
f32 = jnp.float32


def dot32(left, right):
    return jnp.dot(left, right, preferred_element_type=f32)


def dot_t(left, right):
    return lax.dot_general(left, right, (((1,), (1,)), ((), ())), preferred_element_type=f32)


def t_dot(left, right):
    return lax.dot_general(left, right, (((0,), (0,)), ((), ())), preferred_element_type=f32)


def rope_tables(position):
    half_dim = HEAD_DIM // 2
    steps_f = jnp.arange(half_dim, dtype=f32)
    frequency = jnp.exp(steps_f * (-2.0 * jnp.log(f32(rope_base)) / HEAD_DIM))
    angles = position.astype(f32)[:, None] * frequency[None, :]
    cosine = jnp.concatenate([jnp.cos(angles), jnp.cos(angles)], axis=1)
    sine = jnp.concatenate([jnp.sin(angles), jnp.sin(angles)], axis=1)
    return (cosine, sine)


def rotate(values, cosine, sine):
    half_dim = values.shape[-1] // 2
    turned = jnp.concatenate([-values[..., half_dim:], values[..., :half_dim]], axis=-1)
    return values * cosine[:, None, :] + turned * sine[:, None, :]


def rotate_back(grad_in, cosine, sine):
    half_dim = grad_in.shape[-1] // 2
    shifted = grad_in * sine[:, None, :]
    turned = jnp.concatenate([shifted[..., half_dim:], -shifted[..., :half_dim]], axis=-1)
    return grad_in * cosine[:, None, :] + turned


def normalize(values, gain):
    norm_scale = lax.rsqrt(jnp.mean(values * values, axis=-1, keepdims=True) + epsilon)
    plain = values * norm_scale
    return (plain, norm_scale, plain * gain.astype(f32)[None, :])


def norm_back(d_out, plain, norm_scale, gain):
    gain_grad = jnp.sum(d_out * plain, axis=0)
    scaled = d_out * gain.astype(f32)[None, :]
    d_in = norm_scale * (scaled - plain * jnp.mean(scaled * plain, axis=-1, keepdims=True))
    return (d_in, gain_grad)


def make_body(nc, nf):
    nz = nc // 2
    power = nz & (nz - 1) == 0
    fpower = nf & (nf - 1) == 0
    swap_pairs = [(i, i ^ 1) for i in range(nc)]
    z_groups = [[2 * z + k for z in range(nz)] for k in range(2)]

    def step_to(at, d, n, pow2):
        return at ^ d if pow2 else (at + d) % n

    def step_from(at, d, n, pow2):
        return at ^ d if pow2 else (at + n - d) % n

    def swap(x):
        return lax.ppermute(x, "ctx", swap_pairs)

    def send_z(x, d):
        pairs = [(2 * z + k, 2 * step_to(z, d, nz, power) + k) for z in range(nz) for k in range(2)]
        return lax.ppermute(x, "ctx", pairs)

    def send_f(x, d):
        return lax.ppermute(x, "fsdp", [(i, step_to(i, d, nf, fpower)) for i in range(nf)])

    def gather_z(x, z):
        out = jnp.zeros((nz,) + x.shape, x.dtype)
        out = lax.dynamic_update_index_in_dim(out, x, z, 0)
        for d in range(1, nz):
            out = lax.dynamic_update_index_in_dim(out, send_z(x, d), step_from(z, d, nz, power), 0)
        return out

    def gather_f(x, f):
        out = jnp.zeros((nf,) + x.shape, x.dtype)
        out = lax.dynamic_update_index_in_dim(out, x, f, 0)
        for d in range(1, nf):
            out = lax.dynamic_update_index_in_dim(out, send_f(x, d), step_from(f, d, nf, fpower), 0)
        return out

    def scatter_z(x, z):
        total = lax.dynamic_index_in_dim(x, z, 0, keepdims=False)
        for d in range(1, nz):
            piece = lax.dynamic_index_in_dim(x, step_to(z, d, nz, power), 0, keepdims=False)
            total = total + send_z(piece.astype(bf16), d).astype(f32)
        return total

    def scatter_f(x, f):
        total = lax.dynamic_index_in_dim(x, f, 0, keepdims=False)
        for d in range(1, nf):
            piece = lax.dynamic_index_in_dim(x, step_to(f, d, nf, fpower), 0, keepdims=False)
            total = total + send_f(piece.astype(bf16), d).astype(f32)
        return total

    def a2a_f(x):
        return lax.all_to_all(x, "fsdp", 0, 0, tiled=True)

    def a2a_z(x):
        return lax.all_to_all(x, "ctx", 0, 0, tiled=True, axis_index_groups=z_groups)

    def spread(x, n):
        return jnp.broadcast_to(x[None], (n,) + x.shape)

    def both_cores(own, k, axis):
        other = swap(own)
        first = jnp.where(k == 0, own, other)
        second = jnp.where(k == 0, other, own)
        return jnp.stack([first, second], axis=axis)

    def core_sum(x, k, dtype):
        keep = jnp.where(k == 0, x[:, 0], x[:, 1])
        give = jnp.where(k == 0, x[:, 1], x[:, 0])
        return keep + swap(give.astype(dtype)).astype(f32)

    def body(
        hidden_in,
        positions,
        attn_gain,
        w_query,
        w_key,
        w_value,
        w_out,
        ffn_gain,
        w_gate,
        w_up,
        w_down,
        cotangent,
    ):
        x_in = hidden_in[0]
        local_pos = positions[0]
        cot = cotangent[0]
        rows, width = x_in.shape
        dr = w_query.shape[0]
        kvd = w_key.shape[1]
        heads = w_query.shape[1] // HEAD_DIM
        kv_heads = kvd // HEAD_DIM
        group = heads // kv_heads
        factor = HEAD_DIM ** (-0.5)
        qkv = w_query.shape[1] + 2 * kvd
        fr = w_down.shape[0]
        hid = nc * fr
        main = hid // 128 * 128
        tail = hid - main
        ctx = lax.axis_index("ctx")
        f = lax.axis_index("fsdp")
        z = ctx // 2
        k = ctx % 2

        w_attn = jnp.concatenate([w_query, w_key, w_value], axis=1)
        attn_z = gather_z(w_attn, z)
        gains = lax.all_to_all(
            jnp.broadcast_to(jnp.concatenate([attn_gain, ffn_gain])[None], (nc * nf, 2 * dr)),
            ("ctx", "fsdp"), 0, 0, tiled=True)
        gain_a = gains[:, :dr].reshape(width)
        gain_f = gains[:, dr:].reshape(width)
        attn_f = a2a_f(spread(attn_z, nf))
        attn_full = both_cores(attn_f, k, 0).transpose(2, 0, 1, 3, 4).reshape(width, qkv)

        def columns(w):
            return w.reshape(dr, nc, nf, fr).transpose(2, 0, 1, 3).reshape(nf, dr, hid)

        def packed(a, b):
            return jnp.concatenate([a[..., :main], b[..., :main], a[..., main:], b[..., main:]], axis=-1)

        def unpacked(p):
            return (
                jnp.concatenate([p[..., :main], p[..., 2 * main:2 * main + tail]], axis=-1),
                jnp.concatenate([p[..., main:2 * main], p[..., 2 * main + tail:]], axis=-1),
            )

        w_in = a2a_f(packed(columns(w_gate), columns(w_up))).reshape(nf * dr, 2 * hid)

        resid_in = x_in.astype(f32)
        plain_a, scale_a, normed_a = normalize(resid_in, gain_a)
        normed_b = normed_a.astype(bf16)
        cosine, sine = rope_tables(local_pos)
        proj = dot32(normed_b, attn_full)
        queries = rotate(proj[:, :width].reshape(rows, heads, HEAD_DIM), cosine, sine).astype(bf16)
        q_heads = queries.reshape(rows, kv_heads, group, HEAD_DIM)
        keys_local = (
            rotate(proj[:, width:width + kvd].reshape(rows, kv_heads, HEAD_DIM), cosine, sine)
            .astype(bf16)
            .reshape(rows, kvd)
        )
        values_local = proj[:, width + kvd:].astype(bf16)

        high = (local_pos // 64).astype(bf16)
        low = (local_pos % 64).astype(bf16)
        extra = jnp.pad(jnp.stack([high, low]), ((0, 14), (0, 2 * kvd - rows)))
        kv_own = jnp.concatenate([jnp.concatenate([keys_local, values_local], axis=1), extra], axis=0)
        kv_z = a2a_z(spread(kv_own, nz))
        kv_all = jnp.stack([kv_z, swap(kv_z)])
        length = nc * rows
        keys_all = kv_all[:, :, :rows, :kvd].reshape(length, kv_heads, HEAD_DIM)
        values_all = kv_all[:, :, :rows, kvd:].reshape(length, kv_heads, HEAD_DIM)
        key_pos = (kv_all[:, :, rows, :rows].astype(f32) * 64.0 + kv_all[:, :, rows + 1, :rows].astype(f32)).reshape(length)

        w_in_z = gather_z(w_in, z)
        w_down_z = gather_z(w_down, z)
        w_out_z = gather_z(w_out, z)
        cot_g = gather_f(cot, f).reshape(nf * rows, width)
        w_out_f = gather_f(w_out_z, f)
        out_full = both_cores(w_out_f, k, 0).transpose(2, 0, 1, 3, 4).reshape(width, width)
        w_in_full = both_cores(w_in_z, k, 1).reshape(width, 2 * hid)
        w_down_full = both_cores(w_down_z, k, 1).reshape(hid, width)

        allowed = (key_pos[None, :] <= local_pos.astype(f32)[:, None])[None, None]

        def scores_of(q, keys):
            s = jnp.einsum("qkgd,lkd->kgql", q, keys, preferred_element_type=f32) * factor
            return jnp.where(allowed, s, masked_score)

        scores = scores_of(q_heads, keys_all)
        highest = jnp.max(scores, axis=-1, keepdims=True)
        summed = jnp.sum(jnp.where(allowed, jnp.exp(scores - highest), 0.0), axis=-1, keepdims=True)
        log_total = highest + jnp.log(summed)
        probs = jnp.where(allowed, jnp.exp(scores - log_total), 0.0).astype(bf16)
        attn_heads = jnp.einsum("kgql,lkd->qkgd", probs, values_all, preferred_element_type=f32).astype(bf16)
        attn_flat = attn_heads.reshape(rows, width)
        resid_mid = resid_in + dot32(attn_flat, out_full)
        plain_f, scale_f, normed_f = normalize(resid_mid, gain_f)
        normed_h = a2a_f(spread(normed_f.astype(bf16), nf)).reshape(nf * rows, width)

        gate, up = unpacked(dot32(normed_h, w_in_full))
        sig = jax.nn.sigmoid(gate)
        silu = gate * sig
        activation = (silu * up).astype(bf16)
        act_grad = dot_t(cot_g, w_down_full)
        up_grad = (act_grad * silu).astype(bf16)
        gate_grad = (act_grad * up * sig * (1.0 + gate * (1.0 - sig))).astype(bf16)
        in_grad = packed(gate_grad, up_grad)
        normed_part = dot_t(in_grad, w_in_full)
        normed_grad = jnp.sum(a2a_f(normed_part.reshape(nf, rows, width)), axis=0)

        block_part = dot32(activation, w_down_full).reshape(nf, rows, width)
        block_out = resid_mid + scatter_f(block_part, f)

        w_in_part = t_dot(normed_h, in_grad).reshape(nz, 2, nf * dr, 2 * hid)
        w_down_part = t_dot(activation, cot_g).reshape(nz, 2, fr, width)
        w_in_sum = scatter_z(core_sum(w_in_part, k, f32), z)
        w_down_grad = scatter_z(core_sum(w_down_part, k, f32), z)

        mid_norm_grad, ffn_gain_grad = norm_back(normed_grad, plain_f, scale_f, gain_f)
        mid_grad = cot.astype(f32) + mid_norm_grad
        mid_grad_b = mid_grad.astype(bf16)
        attn_grad = dot_t(mid_grad_b, out_full).astype(bf16).reshape(rows, kv_heads, group, HEAD_DIM)
        delta = jnp.einsum("qkgd,qkgd->kgq", attn_grad, attn_heads, preferred_element_type=f32)

        scores2 = scores_of(q_heads, keys_all)
        probs_f = jnp.where(allowed, jnp.exp(scores2 - log_total), 0.0)
        value_grad = jnp.einsum("kgql,qkgd->lkd", probs_f.astype(bf16), attn_grad, preferred_element_type=f32)
        d_probs = jnp.einsum("qkgd,lkd->kgql", attn_grad, values_all, preferred_element_type=f32)
        d_scores = (probs_f * (d_probs - delta[..., None]) * factor).astype(bf16)
        query_grad = jnp.einsum("kgql,lkd->qkgd", d_scores, keys_all, preferred_element_type=f32)
        key_grad = jnp.einsum("kgql,qkgd->lkd", d_scores, q_heads, preferred_element_type=f32)
        kv_part = jnp.concatenate([key_grad.reshape(length, kvd), value_grad.reshape(length, kvd)], axis=1)
        kv_part = kv_part.reshape(2, nz, rows, 2 * kvd)
        kv_sum = kv_part[0] + swap(kv_part[1])
        kv_grad = jnp.sum(a2a_z(kv_sum), axis=0)

        query_grad_b = (
            rotate_back(query_grad.reshape(rows, heads, HEAD_DIM), cosine, sine)
            .astype(bf16)
            .reshape(rows, width)
        )
        key_grad_b = (
            rotate_back(kv_grad[:, :kvd].reshape(rows, kv_heads, HEAD_DIM), cosine, sine)
            .astype(bf16)
            .reshape(rows, kvd)
        )
        value_grad_b = kv_grad[:, kvd:].astype(bf16)
        proj_grad = jnp.concatenate([query_grad_b, key_grad_b, value_grad_b], axis=1)
        input_norm_grad = dot_t(proj_grad, attn_full)
        in_norm_grad, attn_gain_grad = norm_back(input_norm_grad, plain_a, scale_a, gain_a)
        input_grad = mid_grad + in_norm_grad

        def reduce_all(part, cols):
            part = part.reshape(nz, 2, nf, dr, cols).transpose(2, 1, 0, 3, 4)
            part = core_sum(part, k, f32)
            part = scatter_f(part, f)
            return scatter_z(part, z)

        w_out_grad = reduce_all(t_dot(attn_flat, mid_grad_b), width)
        w_attn_grad = reduce_all(t_dot(normed_b, proj_grad), qkv)

        gain_parts = jnp.concatenate(
            [attn_gain_grad.reshape(nc * nf, dr), ffn_gain_grad.reshape(nc * nf, dr)], axis=1)
        gain_grads = jnp.sum(
            lax.all_to_all(gain_parts, ("ctx", "fsdp"), 0, 0, tiled=True), axis=0)

        w_in_rows = a2a_f(w_in_sum.reshape(nf, dr, 2 * hid))

        def owner_columns(p):
            return p.reshape(nf, dr, nc, fr).transpose(1, 2, 0, 3).reshape(dr, nc * nf * fr)

        gate_cols, up_cols = unpacked(w_in_rows)
        return (
            block_out[None],
            input_grad[None],
            gain_grads[:dr],
            w_attn_grad[:, :width],
            w_attn_grad[:, width:width + kvd],
            w_attn_grad[:, width + kvd:],
            w_out_grad,
            gain_grads[dr:],
            owner_columns(gate_cols),
            owner_columns(up_cols),
            w_down_grad,
        )

    return body


def solution(mesh):
    tokens = P("fsdp", "ctx", None)
    shard = P(("ctx", "fsdp"))
    shard2 = P(("ctx", "fsdp"), None)
    return jax.shard_map(
        make_body(mesh.shape["ctx"], mesh.shape["fsdp"]),
        mesh=mesh,
        in_specs=(tokens, P("fsdp", "ctx"), shard, shard2, shard2, shard2, shard2, shard,
                  shard2, shard2, shard2, tokens),
        out_specs=(tokens, tokens, shard, shard2, shard2, shard2, shard2, shard,
                   shard2, shard2, shard2),
        check_vma=False,
    )
```

```python
import jax
import jax.numpy as jnp
from jax import lax
from jax.experimental import pallas as pl
from jax.experimental.pallas import tpu as pltpu
from jax.sharding import PartitionSpec as P

HEAD_DIM = 64

epsilon = 1e-05
rope_base = 10000.0
masked_score = -1e30
bf16 = jnp.bfloat16
f32 = jnp.float32


def dot32(left, right):
    return jnp.dot(left, right, preferred_element_type=f32)


def dot_t(left, right):
    return lax.dot_general(left, right, (((1,), (1,)), ((), ())), preferred_element_type=f32)


def t_dot(left, right):
    return lax.dot_general(left, right, (((0,), (0,)), ((), ())), preferred_element_type=f32)


def rope_tables(position):
    half_dim = HEAD_DIM // 2
    steps_f = jnp.arange(half_dim, dtype=f32)
    frequency = jnp.exp(steps_f * (-2.0 * jnp.log(f32(rope_base)) / HEAD_DIM))
    angles = position.astype(f32)[:, None] * frequency[None, :]
    cosine = jnp.concatenate([jnp.cos(angles), jnp.cos(angles)], axis=1)
    sine = jnp.concatenate([jnp.sin(angles), jnp.sin(angles)], axis=1)
    return (cosine, sine)


def rotate(values, cosine, sine):
    half_dim = values.shape[-1] // 2
    turned = jnp.concatenate([-values[..., half_dim:], values[..., :half_dim]], axis=-1)
    return values * cosine[:, None, :] + turned * sine[:, None, :]


def rotate_back(grad_in, cosine, sine):
    half_dim = grad_in.shape[-1] // 2
    shifted = grad_in * sine[:, None, :]
    turned = jnp.concatenate([shifted[..., half_dim:], -shifted[..., :half_dim]], axis=-1)
    return grad_in * cosine[:, None, :] + turned


def normalize(values, gain):
    norm_scale = lax.rsqrt(jnp.mean(values * values, axis=-1, keepdims=True) + epsilon)
    plain = values * norm_scale
    return (plain, norm_scale, plain * gain.astype(f32)[None, :])


def norm_back(d_out, plain, norm_scale, gain):
    gain_grad = jnp.sum(d_out * plain, axis=0)
    scaled = d_out * gain.astype(f32)[None, :]
    d_in = norm_scale * (scaled - plain * jnp.mean(scaled * plain, axis=-1, keepdims=True))
    return (d_in, gain_grad)


def general_body(nc, nf):
    nz = nc // 2
    power = nz & (nz - 1) == 0
    fpower = nf & (nf - 1) == 0
    swap_pairs = [(i, i ^ 1) for i in range(nc)]
    z_groups = [[2 * z + k for z in range(nz)] for k in range(2)]

    def step_to(at, d, n, pow2):
        return at ^ d if pow2 else (at + d) % n

    def step_from(at, d, n, pow2):
        return at ^ d if pow2 else (at + n - d) % n

    def swap(x):
        return lax.ppermute(x, "ctx", swap_pairs)

    def send_z(x, d):
        pairs = [(2 * z + k, 2 * step_to(z, d, nz, power) + k) for z in range(nz) for k in range(2)]
        return lax.ppermute(x, "ctx", pairs)

    def send_f(x, d):
        return lax.ppermute(x, "fsdp", [(i, step_to(i, d, nf, fpower)) for i in range(nf)])

    def gather_z(x, z):
        out = jnp.zeros((nz,) + x.shape, x.dtype)
        out = lax.dynamic_update_index_in_dim(out, x, z, 0)
        for d in range(1, nz):
            out = lax.dynamic_update_index_in_dim(out, send_z(x, d), step_from(z, d, nz, power), 0)
        return out

    def gather_f(x, f):
        out = jnp.zeros((nf,) + x.shape, x.dtype)
        out = lax.dynamic_update_index_in_dim(out, x, f, 0)
        for d in range(1, nf):
            out = lax.dynamic_update_index_in_dim(out, send_f(x, d), step_from(f, d, nf, fpower), 0)
        return out

    def scatter_z(x, z):
        total = lax.dynamic_index_in_dim(x, z, 0, keepdims=False)
        for d in range(1, nz):
            piece = lax.dynamic_index_in_dim(x, step_to(z, d, nz, power), 0, keepdims=False)
            total = total + send_z(piece.astype(bf16), d).astype(f32)
        return total

    def scatter_f(x, f):
        total = lax.dynamic_index_in_dim(x, f, 0, keepdims=False)
        for d in range(1, nf):
            piece = lax.dynamic_index_in_dim(x, step_to(f, d, nf, fpower), 0, keepdims=False)
            total = total + send_f(piece.astype(bf16), d).astype(f32)
        return total

    def a2a_f(x):
        return lax.all_to_all(x, "fsdp", 0, 0, tiled=True)

    def a2a_z(x):
        return lax.all_to_all(x, "ctx", 0, 0, tiled=True, axis_index_groups=z_groups)

    def spread(x, n):
        return jnp.broadcast_to(x[None], (n,) + x.shape)

    def both_cores(own, k, axis):
        other = swap(own)
        first = jnp.where(k == 0, own, other)
        second = jnp.where(k == 0, other, own)
        return jnp.stack([first, second], axis=axis)

    def core_sum(x, k, dtype):
        keep = jnp.where(k == 0, x[:, 0], x[:, 1])
        give = jnp.where(k == 0, x[:, 1], x[:, 0])
        return keep + swap(give.astype(dtype)).astype(f32)

    def body(
        hidden_in,
        positions,
        attn_gain,
        w_query,
        w_key,
        w_value,
        w_out,
        ffn_gain,
        w_gate,
        w_up,
        w_down,
        cotangent,
    ):
        x_in = hidden_in[0]
        local_pos = positions[0]
        cot = cotangent[0]
        rows, width = x_in.shape
        dr = w_query.shape[0]
        kvd = w_key.shape[1]
        heads = w_query.shape[1] // HEAD_DIM
        kv_heads = kvd // HEAD_DIM
        group = heads // kv_heads
        factor = HEAD_DIM ** (-0.5)
        qkv = w_query.shape[1] + 2 * kvd
        fr = w_down.shape[0]
        hid = nc * fr
        main = hid // 128 * 128
        tail = hid - main
        ctx = lax.axis_index("ctx")
        f = lax.axis_index("fsdp")
        z = ctx // 2
        k = ctx % 2

        w_attn = jnp.concatenate([w_query, w_key, w_value], axis=1)
        attn_z = gather_z(w_attn, z)
        gains = lax.all_to_all(
            jnp.broadcast_to(jnp.concatenate([attn_gain, ffn_gain])[None], (nc * nf, 2 * dr)),
            ("ctx", "fsdp"), 0, 0, tiled=True)
        gain_a = gains[:, :dr].reshape(width)
        gain_f = gains[:, dr:].reshape(width)
        attn_f = a2a_f(spread(attn_z, nf))
        attn_full = both_cores(attn_f, k, 0).transpose(2, 0, 1, 3, 4).reshape(width, qkv)

        def columns(w):
            return w.reshape(dr, nc, nf, fr).transpose(2, 0, 1, 3).reshape(nf, dr, hid)

        def packed(a, b):
            return jnp.concatenate([a[..., :main], b[..., :main], a[..., main:], b[..., main:]], axis=-1)

        def unpacked(p):
            return (
                jnp.concatenate([p[..., :main], p[..., 2 * main:2 * main + tail]], axis=-1),
                jnp.concatenate([p[..., main:2 * main], p[..., 2 * main + tail:]], axis=-1),
            )

        w_in = a2a_f(packed(columns(w_gate), columns(w_up))).reshape(nf * dr, 2 * hid)

        resid_in = x_in.astype(f32)
        plain_a, scale_a, normed_a = normalize(resid_in, gain_a)
        normed_b = normed_a.astype(bf16)
        cosine, sine = rope_tables(local_pos)
        proj = dot32(normed_b, attn_full)
        queries = rotate(proj[:, :width].reshape(rows, heads, HEAD_DIM), cosine, sine).astype(bf16)
        q_heads = queries.reshape(rows, kv_heads, group, HEAD_DIM)
        keys_local = (
            rotate(proj[:, width:width + kvd].reshape(rows, kv_heads, HEAD_DIM), cosine, sine)
            .astype(bf16)
            .reshape(rows, kvd)
        )
        values_local = proj[:, width + kvd:].astype(bf16)

        high = (local_pos // 64).astype(bf16)
        low = (local_pos % 64).astype(bf16)
        extra = jnp.pad(jnp.stack([high, low]), ((0, 14), (0, 2 * kvd - rows)))
        kv_own = jnp.concatenate([jnp.concatenate([keys_local, values_local], axis=1), extra], axis=0)
        kv_z = a2a_z(spread(kv_own, nz))
        kv_all = jnp.stack([kv_z, swap(kv_z)])
        length = nc * rows
        keys_all = kv_all[:, :, :rows, :kvd].reshape(length, kv_heads, HEAD_DIM)
        values_all = kv_all[:, :, :rows, kvd:].reshape(length, kv_heads, HEAD_DIM)
        key_pos = (kv_all[:, :, rows, :rows].astype(f32) * 64.0 + kv_all[:, :, rows + 1, :rows].astype(f32)).reshape(length)

        w_in_z = gather_z(w_in, z)
        w_down_z = gather_z(w_down, z)
        w_out_z = gather_z(w_out, z)
        cot_g = gather_f(cot, f).reshape(nf * rows, width)
        w_out_f = gather_f(w_out_z, f)
        out_full = both_cores(w_out_f, k, 0).transpose(2, 0, 1, 3, 4).reshape(width, width)
        w_in_full = both_cores(w_in_z, k, 1).reshape(width, 2 * hid)
        w_down_full = both_cores(w_down_z, k, 1).reshape(hid, width)

        allowed = (key_pos[None, :] <= local_pos.astype(f32)[:, None])[None, None]

        def scores_of(q, keys):
            s = jnp.einsum("qkgd,lkd->kgql", q, keys, preferred_element_type=f32) * factor
            return jnp.where(allowed, s, masked_score)

        scores = scores_of(q_heads, keys_all)
        highest = jnp.max(scores, axis=-1, keepdims=True)
        summed = jnp.sum(jnp.where(allowed, jnp.exp(scores - highest), 0.0), axis=-1, keepdims=True)
        log_total = highest + jnp.log(summed)
        probs = jnp.where(allowed, jnp.exp(scores - log_total), 0.0).astype(bf16)
        attn_heads = jnp.einsum("kgql,lkd->qkgd", probs, values_all, preferred_element_type=f32).astype(bf16)
        attn_flat = attn_heads.reshape(rows, width)
        resid_mid = resid_in + dot32(attn_flat, out_full)
        plain_f, scale_f, normed_f = normalize(resid_mid, gain_f)
        normed_h = a2a_f(spread(normed_f.astype(bf16), nf)).reshape(nf * rows, width)

        gate, up = unpacked(dot32(normed_h, w_in_full))
        sig = jax.nn.sigmoid(gate)
        silu = gate * sig
        activation = (silu * up).astype(bf16)
        act_grad = dot_t(cot_g, w_down_full)
        up_grad = (act_grad * silu).astype(bf16)
        gate_grad = (act_grad * up * sig * (1.0 + gate * (1.0 - sig))).astype(bf16)
        in_grad = packed(gate_grad, up_grad)
        normed_part = dot_t(in_grad, w_in_full)
        normed_grad = jnp.sum(a2a_f(normed_part.reshape(nf, rows, width)), axis=0)

        block_part = dot32(activation, w_down_full).reshape(nf, rows, width)
        block_out = resid_mid + scatter_f(block_part, f)

        w_in_part = t_dot(normed_h, in_grad).reshape(nz, 2, nf * dr, 2 * hid)
        w_down_part = t_dot(activation, cot_g).reshape(nz, 2, fr, width)
        w_in_sum = scatter_z(core_sum(w_in_part, k, f32), z)
        w_down_grad = scatter_z(core_sum(w_down_part, k, f32), z)

        mid_norm_grad, ffn_gain_grad = norm_back(normed_grad, plain_f, scale_f, gain_f)
        mid_grad = cot.astype(f32) + mid_norm_grad
        mid_grad_b = mid_grad.astype(bf16)
        attn_grad = dot_t(mid_grad_b, out_full).astype(bf16).reshape(rows, kv_heads, group, HEAD_DIM)
        delta = jnp.einsum("qkgd,qkgd->kgq", attn_grad, attn_heads, preferred_element_type=f32)

        scores2 = scores_of(q_heads, keys_all)
        probs_f = jnp.where(allowed, jnp.exp(scores2 - log_total), 0.0)
        value_grad = jnp.einsum("kgql,qkgd->lkd", probs_f.astype(bf16), attn_grad, preferred_element_type=f32)
        d_probs = jnp.einsum("qkgd,lkd->kgql", attn_grad, values_all, preferred_element_type=f32)
        d_scores = (probs_f * (d_probs - delta[..., None]) * factor).astype(bf16)
        query_grad = jnp.einsum("kgql,lkd->qkgd", d_scores, keys_all, preferred_element_type=f32)
        key_grad = jnp.einsum("kgql,qkgd->lkd", d_scores, q_heads, preferred_element_type=f32)
        kv_part = jnp.concatenate([key_grad.reshape(length, kvd), value_grad.reshape(length, kvd)], axis=1)
        kv_part = kv_part.reshape(2, nz, rows, 2 * kvd)
        kv_sum = kv_part[0] + swap(kv_part[1])
        kv_grad = jnp.sum(a2a_z(kv_sum), axis=0)

        query_grad_b = (
            rotate_back(query_grad.reshape(rows, heads, HEAD_DIM), cosine, sine)
            .astype(bf16)
            .reshape(rows, width)
        )
        key_grad_b = (
            rotate_back(kv_grad[:, :kvd].reshape(rows, kv_heads, HEAD_DIM), cosine, sine)
            .astype(bf16)
            .reshape(rows, kvd)
        )
        value_grad_b = kv_grad[:, kvd:].astype(bf16)
        proj_grad = jnp.concatenate([query_grad_b, key_grad_b, value_grad_b], axis=1)
        input_norm_grad = dot_t(proj_grad, attn_full)
        in_norm_grad, attn_gain_grad = norm_back(input_norm_grad, plain_a, scale_a, gain_a)
        input_grad = mid_grad + in_norm_grad

        def reduce_all(part, cols):
            part = part.reshape(nz, 2, nf, dr, cols).transpose(2, 1, 0, 3, 4)
            part = core_sum(part, k, f32)
            part = scatter_f(part, f)
            return scatter_z(part, z)

        w_out_grad = reduce_all(t_dot(attn_flat, mid_grad_b), width)
        w_attn_grad = reduce_all(t_dot(normed_b, proj_grad), qkv)

        gain_parts = jnp.concatenate(
            [attn_gain_grad.reshape(nc * nf, dr), ffn_gain_grad.reshape(nc * nf, dr)], axis=1)
        gain_grads = jnp.sum(
            lax.all_to_all(gain_parts, ("ctx", "fsdp"), 0, 0, tiled=True), axis=0)

        w_in_rows = a2a_f(w_in_sum.reshape(nf, dr, 2 * hid))

        def owner_columns(p):
            return p.reshape(nf, dr, nc, fr).transpose(1, 2, 0, 3).reshape(dr, nc * nf * fr)

        gate_cols, up_cols = unpacked(w_in_rows)
        return (
            block_out[None],
            input_grad[None],
            gain_grads[:dr],
            w_attn_grad[:, :width],
            w_attn_grad[:, width:width + kvd],
            w_attn_grad[:, width + kvd:],
            w_out_grad,
            gain_grads[dr:],
            owner_columns(gate_cols),
            owner_columns(up_cols),
            w_down_grad,
        )

    return body


VMEM = pl.BlockSpec(memory_space=pltpu.VMEM)
SMEM = pl.BlockSpec(memory_space=pltpu.SMEM)


def sds(shape, dtype):
    return jax.ShapeDtypeStruct(shape, dtype)


def size_of(x):
    return x.size * jnp.dtype(x.dtype).itemsize


def call(kernel, ids, ins, outs, scratch=(), flops=0, name=None):
    flat_in, in_tree = jax.tree.flatten(ins)
    flat_out, out_tree = jax.tree.flatten(outs)
    moved = sum(size_of(x) for x in flat_in + flat_out)
    held = sum(size_of(x) for x in scratch)

    def run(ids_ref, *refs):
        n, m = len(flat_in), len(flat_out)
        kernel(ids_ref, *jax.tree.unflatten(in_tree, refs[:n]), *jax.tree.unflatten(out_tree, refs[n:n + m]),
               *refs[n + m:])

    got = pl.pallas_call(
        run,
        out_shape=tuple(flat_out),
        in_specs=[SMEM] + [VMEM] * len(flat_in),
        out_specs=tuple([VMEM] * len(flat_out)),
        scratch_shapes=[pltpu.VMEM(x.shape, x.dtype) for x in scratch],
        compiler_params=pltpu.CompilerParams(vmem_limit_bytes=min(60 << 20, moved + held + (16 << 20))),
        cost_estimate=pl.CostEstimate(flops=int(flops), transcendentals=0, bytes_accessed=int(moved)),
        name=name,
    )(ids, *flat_in)
    return jax.tree.unflatten(out_tree, got)


def nn(a, b):
    return lax.dot_general(a, b, (((1,), (0,)), ((), ())), preferred_element_type=f32)


def nt(a, b):
    return lax.dot_general(a, b, (((1,), (1,)), ((), ())), preferred_element_type=f32)


def tn(a, b):
    return lax.dot_general(a, b, (((0,), (0,)), ((), ())), preferred_element_type=f32)


def tiled_fits(nc, nf, dr, fr, rows, kvd):
    frm = fr // 16 * 16
    frt = fr - frm
    nz = nc // 2
    return (
        nz & (nz - 1) == 0 and nf & (nf - 1) == 0
        and dr % 16 == 0 and fr % 8 == 0 and rows == 128 and kvd == 128
        and (nc * frm) % 128 == 0 and (2 * nc * frt) % 128 == 0
    )


def tiled_body(nc, nf, args):
    nz = nc // 2

    def swap(x):
        return lax.ppermute(x, "ctx", [(i, i ^ 1) for i in range(nc)])

    def send_z(x, d):
        return lax.ppermute(x, "ctx", [(i, i ^ (2 * d)) for i in range(nc)])

    def send_f(x, d):
        return lax.ppermute(x, "fsdp", [(i, i ^ d) for i in range(nf)])

    def gather_z(x):
        return [x] + [send_z(x, d) for d in range(1, nz)]

    def gather_f(x):
        return [x] + [send_f(x, d) for d in range(1, nf)]

    (hidden_in, positions, attn_gain, w_query, w_key, w_value, w_out, ffn_gain,
     w_gate, w_up, w_down, cotangent) = args
    x_in = hidden_in[0]
    cot = cotangent[0]
    rows, width = x_in.shape
    dr = w_query.shape[0]
    kvd = w_key.shape[1]
    qd = w_query.shape[1]
    hd = HEAD_DIM
    half = hd // 2
    heads = qd // hd
    kv_heads = kvd // hd
    group = heads // kv_heads
    factor = hd ** (-0.5)
    qkv = qd + 2 * kvd
    cols = qkv + 128
    length = nc * rows
    blk = nf * dr
    fr = w_down.shape[0]
    frm = fr // 16 * 16
    frt = fr - frm
    main = nc * frm
    tail = nc * frt
    hid = main + tail
    xrows = 16
    ctx = lax.axis_index("ctx")
    ids = jnp.stack([ctx % 2, ctx // 2, lax.axis_index("fsdp")]).astype(jnp.int32)

    def assemble(dst, own, oth, ids_ref):
        k, z0, f0 = ids_ref[0], ids_ref[1], ids_ref[2]
        for src, side in ((own, k), (oth, 1 - k)):
            for d in range(nf):
                for e in range(nz):
                    at = ((z0 ^ e) * 2 + side) * blk + (f0 ^ d) * dr
                    dst[pl.ds(pl.multiple_of(at, 16), dr), :] = src[d][e]

    def column(row):
        n = row.shape[1]
        a = lax.broadcasted_iota(jnp.int32, (n, n), 0)
        b = lax.broadcasted_iota(jnp.int32, (n, n), 1)
        return jnp.sum(jnp.where(a == b, jnp.broadcast_to(row, (n, n)), 0.0), axis=1, keepdims=True)

    def pack_kernel(ids_ref, wq, wk, wv, ga, gf, wa):
        lane = lax.broadcasted_iota(jnp.int32, (dr, 128), 1)
        a = column(ga[...].astype(f32))
        b = column(gf[...].astype(f32))
        wa[:, :qd] = wq[...]
        wa[:, qd:qd + kvd] = wk[...]
        wa[:, qd + kvd:qkv] = wv[...]
        wa[:, qkv:] = jnp.where(lane == 0, a, jnp.where(lane == 1, b, 0.0)).astype(bf16)

    (wa,) = call(pack_kernel, ids, [w_query, w_key, w_value, attn_gain[None], ffn_gain[None]],
                 [sds((dr, cols), bf16)], name="pack")
    attn_own = gather_f(jnp.stack(gather_z(wa)))
    attn_oth = [swap(p) for p in attn_own]

    def pack_in_kernel(ids_ref, wg, wu, wi, s):
        for j in range(nf):
            for c in range(nc):
                at = (c * nf + j) * fr
                for w, a, b in ((wg, c * frm, 2 * main + c * frt), (wu, main + c * frm, 2 * main + tail + c * frt)):
                    s[j, :, a:a + frm] = w[:, at:at + frm]
                    if frt:
                        s[j, :, b:b + frt] = w[:, at + frm:at + fr]
        for d in range(nf):
            wi[d][...] = s[ids_ref[2] ^ d]

    (wi,) = call(pack_in_kernel, ids, [w_gate, w_up], [[sds((dr, 2 * hid), bf16)] * nf],
                 scratch=[sds((nf, dr, 2 * hid), bf16)], name="pack_in")

    pos_row = positions.astype(f32)
    steps_f = jnp.arange(half, dtype=f32)
    frequency = jnp.exp(steps_f * (-2.0 * jnp.log(f32(rope_base)) / hd))
    angles = frequency[:, None] * pos_row
    cos_t = jnp.cos(angles)
    sin_t = jnp.sin(angles)
    extra = jnp.pad(
        jnp.concatenate([positions // 64, positions % 64], axis=0).astype(bf16),
        ((0, xrows - 2), (0, 2 * kvd - rows)))

    def proj_kernel(ids_ref, x, own, oth, cos, sin, ext, q_out, kv_out, gain_out, nb_out, w):
        assemble(w, own, oth, ids_ref)
        gains = jnp.transpose(w[:, qkv:].astype(f32))
        gain_out[...] = gains[0:8]
        xf = x[...].astype(f32)
        scale = lax.rsqrt(jnp.mean(xf * xf, axis=-1, keepdims=True) + epsilon)
        normed = xf * scale * gains[0:1]
        nb = normed.astype(bf16)
        nb_out[...] = jnp.transpose(nb.astype(f32)).astype(bf16)
        proj = nn(nb, w[:, :qkv])
        c = cos[...]
        s = sin[...]
        turn = jnp.transpose(proj[:, :qd + kvd])
        for h in range(heads):
            a = turn[h * hd:h * hd + half]
            b = turn[h * hd + half:(h + 1) * hd]
            q_out[h * hd:h * hd + half] = (a * c - b * s).astype(bf16)
            q_out[h * hd + half:(h + 1) * hd] = (b * c + a * s).astype(bf16)
        parts = []
        for h in range(kv_heads):
            a = turn[qd + h * hd:qd + h * hd + half]
            b = turn[qd + h * hd + half:qd + (h + 1) * hd]
            parts += [a * c - b * s, b * c + a * s]
        kv_out[:rows, :kvd] = jnp.transpose(jnp.concatenate(parts, axis=0)).astype(bf16)
        kv_out[:rows, kvd:] = proj[:, qd + kvd:].astype(bf16)
        kv_out[rows:, :] = ext[...]

    q_t, kv_mine, gains, nb_t = call(
        proj_kernel, ids, [x_in, attn_own, attn_oth, cos_t, sin_t, extra],
        [sds((qd, rows), bf16), sds((rows + xrows, 2 * kvd), bf16), sds((8, width), f32), sds((width, rows), bf16)],
        scratch=[sds((width, cols), bf16)], flops=2 * rows * width * qkv, name="proj")

    kv_own = gather_z(kv_mine)
    kv_oth = [swap(p) for p in kv_own]

    w_out_z = jnp.stack(gather_z(w_out))
    out_own = jnp.stack(gather_f(w_out_z))
    out_oth = swap(out_own)
    w_in = jnp.stack([wi[0]] + [send_f(wi[d], d) for d in range(1, nf)])
    w_in_own = jnp.stack(gather_z(w_in))
    w_in_oth = swap(w_in_own)
    w_down_own = jnp.stack(gather_z(w_down))
    w_down_oth = swap(w_down_own)
    cot_all = gather_f(cot)

    def load_keys(own, oth, pos, keys, bias):
        for i in range(nc):
            kv = own[i] if i < nz else oth[i - nz]
            keys[i * rows:(i + 1) * rows, :] = kv[:rows, :]
            ext = jnp.transpose(kv[rows:, :rows].astype(f32))
            kpos = ext[:, 0:1] * 64.0 + ext[:, 1:2]
            bias[i * rows:(i + 1) * rows, :] = jnp.where(kpos <= pos[...], 0.0, masked_score)

    def pair_of(ref, h):
        return jnp.concatenate([ref[h * hd:(h + 1) * hd, :], ref[(h + 1) * hd:(h + 2) * hd, :]], axis=1)

    def attn_kernel(ids_ref, q, kown, koth, pos, x, own, oth, gain, attn_out, lse_out, mid_out, nf_out, w, keys, bias):
        assemble(w, own, oth, ids_ref)
        load_keys(kown, koth, pos, keys, bias)
        b = bias[...]
        bias2 = jnp.concatenate([b, b], axis=1)
        vals_t = jnp.transpose(keys[:, kvd:].astype(f32)).astype(bf16)
        for j in range(kv_heads):
            kj = keys[:, j * hd:(j + 1) * hd]
            vj = vals_t[j * hd:(j + 1) * hd]
            for h in range(j * group, (j + 1) * group, 2):
                s = nn(kj, pair_of(q, h)) * factor + bias2
                high = jnp.max(s, axis=0, keepdims=True)
                e = jnp.exp(s - high)
                total = jnp.sum(e, axis=0, keepdims=True)
                p = (e * (1.0 / total)).astype(bf16)
                lse = high + jnp.log(total)
                o = nn(vj, p).astype(bf16)
                attn_out[h * hd:(h + 1) * hd, :] = o[:, :rows]
                attn_out[(h + 1) * hd:(h + 2) * hd, :] = o[:, rows:]
                lse_out[h:h + 1, :] = lse[:, :rows]
                lse_out[h + 1:h + 2, :] = lse[:, rows:]
        attn = jnp.transpose(attn_out[...].astype(f32)).astype(bf16)
        mid = x[...].astype(f32) + nn(attn, w[...])
        mid_out[...] = mid
        scale = lax.rsqrt(jnp.mean(mid * mid, axis=-1, keepdims=True) + epsilon)
        nf_out[...] = (mid * scale * gain[1:2]).astype(bf16)

    attn_t, lse, mid, nh_mine = call(
        attn_kernel, ids, [q_t, kv_own, kv_oth, pos_row, x_in, out_own, out_oth, gains],
        [sds((qd, rows), bf16), sds((heads, rows), f32), sds((rows, width), f32), sds((rows, width), bf16)],
        scratch=[sds((qd, width), bf16), sds((length, 2 * kvd), bf16), sds((length, rows), f32)],
        flops=4 * heads * rows * length * 128 + 2 * rows * qd * width, name="attn")

    nh_all = gather_f(nh_mine)

    def weights_kernel(ids_ref, iown, ioth, down, doth, wi_out, wd_out):
        k, z0, f0 = ids_ref[0], ids_ref[1], ids_ref[2]
        for src, side in ((iown, k), (ioth, 1 - k)):
            for e in range(nz):
                for d in range(nf):
                    at = ((z0 ^ e) * 2 + side) * blk + (f0 ^ d) * dr
                    wi_out[pl.ds(pl.multiple_of(at, 16), dr), :] = src[e, d]
        for e in range(nz):
            for src, side in ((down, k), (doth, 1 - k)):
                at = ((z0 ^ e) * 2 + side) * frm
                wd_out[pl.ds(pl.multiple_of(at, 16), frm), :] = src[e, :frm]
            if frt:
                mine = down[e, frm:].astype(f32)
                theirs = doth[e, frm:].astype(f32)
                first = jnp.where(k == 0, mine, theirs)
                second = jnp.where(k == 0, theirs, mine)
                wd_out[pl.ds(pl.multiple_of(main + (z0 ^ e) * 2 * frt, 16), 2 * frt), :] = jnp.concatenate(
                    [first, second], axis=0).astype(bf16)

    w_i, w_d = call(weights_kernel, ids, [w_in_own, w_in_oth, w_down_own, w_down_oth],
                    [sds((width, 2 * hid), bf16), sds((hid, width), bf16)], name="weights")

    def ffn_kernel(ids_ref, nh, ct, wi_r, wd_r, act_out, grad_out, part_out):
        g = nn(nh[...], wi_r[...])
        ag = nt(ct[...], wd_r[...])

        def one(gate, up, agn):
            sig = 1.0 / (1.0 + jnp.exp(-gate))
            silu = gate * sig
            return (
                (silu * up).astype(bf16),
                (agn * up * sig * (1.0 + gate * (1.0 - sig))).astype(bf16),
                (agn * silu).astype(bf16),
            )

        a, gg, ug = one(g[:, :main], g[:, main:2 * main], ag[:, :main])
        act_out[:, :main] = a
        grad_out[:, :main] = gg
        grad_out[:, main:2 * main] = ug
        if tail:
            t = g[:, 2 * main:]
            a, gg, ug = one(t[:, :tail], t[:, tail:], ag[:, main:])
            act_out[:, main:] = a
            grad_out[:, 2 * main:] = jnp.concatenate([gg, ug], axis=1)
        part_out[...] = nt(grad_out[...], wi_r[...])

    acts, in_grads, parts = [], [], []
    for d in range(nf):
        a, g, p = call(
            ffn_kernel, ids, [nh_all[d], cot_all[d], w_i, w_d],
            [sds((rows, hid), bf16), sds((rows, 2 * hid), bf16), sds((rows, width), f32)],
            flops=2 * rows * width * 5 * hid, name="ffn")
        acts.append(a)
        in_grads.append(g)
        parts.append(p)
    norm_recv = [parts[0]] + [send_f(parts[d], d) for d in range(1, nf)]

    def ffn_w_kernel(ids_ref, nh, ct, actr, gradr, wd_r, blk_out, in_keep, in_give, dn_keep, dn_give, gd_s):
        k, z0 = ids_ref[0], ids_ref[1]
        act = jnp.concatenate([a[...] for a in actr], axis=0)
        out = nn(act, wd_r[...])
        blk_out[0][...] = out[:rows]
        for d in range(1, nf):
            blk_out[d][...] = out[d * rows:(d + 1) * rows].astype(bf16)
        nh2 = jnp.concatenate([a[...] for a in nh], axis=0)
        ct2 = jnp.concatenate([a[...] for a in ct], axis=0)
        gr2 = jnp.concatenate([a[...] for a in gradr], axis=0)
        for c in range(nc):
            g = tn(nh2[:, c * blk:(c + 1) * blk], gr2)

            @pl.when(k == c % 2)
            def _():
                in_keep[(c // 2) ^ z0] = g

            @pl.when(k != c % 2)
            def _():
                in_give[(c // 2) ^ z0] = g
        gd_s[...] = tn(act, ct2)
        for out_r, side in ((dn_keep, k), (dn_give, 1 - k)):
            for e in range(nz):
                at = (z0 ^ e) * 2 + side
                out_r[e, :frm, :] = gd_s[pl.ds(pl.multiple_of(at * frm, 8), frm), :]
                if frt:
                    out_r[e, frm:, :] = gd_s[pl.ds(pl.multiple_of(main + at * frt, 8), frt), :]

    blk_own, in_keep, in_give, dn_keep, dn_give = call(
        ffn_w_kernel, ids, [nh_all, cot_all, acts, in_grads, w_d],
        [[sds((rows, width), f32)] + [sds((rows, width), bf16)] * (nf - 1),
         sds((nz, blk, 2 * hid), f32), sds((nz, blk, 2 * hid), f32),
         sds((nz, fr, width), f32), sds((nz, fr, width), f32)],
        scratch=[sds((hid, width), f32)], flops=2 * nf * rows * width * 4 * hid, name="ffn_w")

    blk_recv = [send_f(blk_own[d], d) for d in range(1, nf)]
    block_out = mid + blk_own[0]
    for p in blk_recv:
        block_out = block_out + p.astype(f32)

    def mid_kernel(ids_ref, npart, midr, ct, gain, own, oth, mg_out, mgb_out, do_out, fg_out, w):
        assemble(w, own, oth, ids_ref)
        m = midr[...]
        scale = lax.rsqrt(jnp.mean(m * m, axis=-1, keepdims=True) + epsilon)
        plain = m * scale
        ng = npart[0][...]
        for i in range(1, nf):
            ng = ng + npart[i][...]
        fg_out[...] = jnp.broadcast_to(jnp.sum(ng * plain, axis=0, keepdims=True), (8, width))
        e = ng * gain[1:2]
        mg = ct[...].astype(f32) + scale * (e - plain * jnp.mean(e * plain, axis=-1, keepdims=True))
        mg_out[...] = mg
        mgb = mg.astype(bf16)
        mgb_out[...] = mgb
        do_out[...] = jnp.transpose(nt(mgb, w[...]).astype(bf16).astype(f32)).astype(bf16)

    mid_grad, mgb, do_t, fg = call(
        mid_kernel, ids, [norm_recv, mid, cot, gains, out_own, out_oth],
        [sds((rows, width), f32), sds((rows, width), bf16), sds((qd, rows), bf16), sds((8, width), f32)],
        scratch=[sds((qd, width), bf16)], flops=2 * rows * qd * width, name="mid")

    def back_kernel(ids_ref, do_t, q, kown, koth, pos, attn, lse_r, cos, sin,
                    dq_out, kv_keep, kv_give, keys, bias, dq_t):
        load_keys(kown, koth, pos, keys, bias)
        b = bias[...]
        bias2 = jnp.concatenate([b, b], axis=1)
        keys_t = jnp.transpose(keys[:, :kvd].astype(f32)).astype(bf16)
        for j in range(kv_heads):
            kj = keys[:, j * hd:(j + 1) * hd]
            vj = keys[:, kvd + j * hd:kvd + (j + 1) * hd]
            ktj = keys_t[j * hd:(j + 1) * hd]
            dk = None
            dv = None
            for h in range(j * group, (j + 1) * group, 2):
                qp = pair_of(q, h)
                dop = pair_of(do_t, h)
                op = pair_of(attn, h)
                delta = jnp.sum(dop.astype(f32) * op.astype(f32), axis=0, keepdims=True)
                lsep = jnp.concatenate([lse_r[h:h + 1, :], lse_r[h + 1:h + 2, :]], axis=1)
                p = jnp.exp(nn(kj, qp) * factor + bias2 - lsep)
                dp = nn(vj, dop)
                ds = (p * (dp - delta) * factor).astype(bf16)
                pv = nt(p.astype(bf16), dop)
                pk = nt(ds, qp)
                dv = pv if dv is None else dv + pv
                dk = pk if dk is None else dk + pk
                dq = nn(ktj, ds)
                dq_t[h * hd:(h + 1) * hd, :] = dq[:, :rows]
                dq_t[(h + 1) * hd:(h + 2) * hd, :] = dq[:, rows:]
            for i in range(nc):
                out = kv_keep if i < nz else kv_give
                out[i % nz, :, j * hd:(j + 1) * hd] = dk[i * rows:(i + 1) * rows]
                out[i % nz, :, kvd + j * hd:kvd + (j + 1) * hd] = dv[i * rows:(i + 1) * rows]
        c = cos[...]
        s = sin[...]
        for h in range(heads):
            a = dq_t[h * hd:h * hd + half, :]
            d = dq_t[h * hd + half:(h + 1) * hd, :]
            dq_t[h * hd:h * hd + half, :] = a * c + d * s
            dq_t[h * hd + half:(h + 1) * hd, :] = d * c - a * s
        dq_out[...] = jnp.transpose(dq_t[...]).astype(bf16)

    dq, kv_keep, kv_give = call(
        back_kernel, ids, [do_t, q_t, kv_own, kv_oth, pos_row, attn_t, lse, cos_t, sin_t],
        [sds((rows, qd), bf16), sds((nz, rows, 2 * kvd), f32), sds((nz, rows, 2 * kvd), f32)],
        scratch=[sds((length, 2 * kvd), bf16), sds((length, rows), f32), sds((qd, rows), f32)],
        flops=10 * heads * rows * length * 128, name="back")

    def add_split_kernel(ids_ref, keep, recv, mine, others):
        n = len(others) + 1
        mine[...] = keep[0] + recv[0]
        for d in range(1, n):
            others[d - 1][...] = (keep[d] + recv[d]).astype(others[d - 1].dtype)

    def add_split(keep, recv, dtype, name):
        n = keep.shape[0]
        piece = keep.shape[1:]
        return call(add_split_kernel, ids, [keep, recv], [sds(piece, f32), [sds(piece, dtype)] * (n - 1)], name=name)

    def merge_split_kernel(ids_ref, mine, recv, first, others):
        for d in range(nz):
            total = mine[d]
            for r in recv:
                total = total + r[d].astype(f32)
            if d == 0:
                first[...] = total
            else:
                others[d - 1][...] = total.astype(bf16)

    def merge_kernel(ids_ref, mine, recv, total):
        t = mine[...]
        for r in recv:
            t = t + r[...].astype(f32)
        total[...] = t

    def merge(mine, recv, name):
        return call(merge_kernel, ids, [mine, recv], [sds(mine.shape, f32)], name=name)[0]

    kv_first, kv_rest = add_split(kv_keep, swap(kv_give), f32, "kv_add")
    kv_recv = [kv_first] + [send_z(kv_rest[d - 1], d) for d in range(1, nz)]

    def split_rows(g, keep, give, ids_ref):
        k, z0, f0 = ids_ref[0], ids_ref[1], ids_ref[2]
        for out, side in ((keep, k), (give, 1 - k)):
            for d in range(nf):
                for e in range(nz):
                    at = ((z0 ^ e) * 2 + side) * blk + (f0 ^ d) * dr
                    out[d, e] = g[pl.ds(pl.multiple_of(at, 8), dr), :]

    def outer_kernel(ids_ref, left, right, keep, give, g):
        g[...] = nn(left[...], right[...])
        split_rows(g, keep, give, ids_ref)

    def outer(left, right, name):
        n = right.shape[1]
        shape = sds((nf, nz, dr, n), f32)
        return call(outer_kernel, ids, [left, right], [shape, shape],
                    scratch=[sds((width, n), f32)], flops=2 * width * rows * n, name=name)

    def reduce_all(keep, give, name):
        mine, others = add_split(keep, swap(give), bf16, name + "_c")
        recv = [send_f(others[d - 1], d) for d in range(1, nf)]
        piece = mine.shape[1:]
        first, rest = call(merge_split_kernel, ids, [mine, recv],
                           [sds(piece, f32), [sds(piece, bf16)] * (nz - 1)], name=name + "_f")
        return merge(first, [send_z(rest[d - 1], d) for d in range(1, nz)], name + "_z")

    w_out_grad = reduce_all(*outer(attn_t, mgb, "out_w"), "out")
    w_query_grad = reduce_all(*outer(nb_t, dq, "query_w"), "query")

    def last_kernel(ids_ref, kvp, dqr, x, nbt, gain, fgr, mgr, own, oth, cos, sin, grad_out, keep, give, w, g):
        assemble(w, own, oth, ids_ref)
        kv = kvp[0][...]
        for i in range(1, nz):
            kv = kv + kvp[i][...]
        c = cos[...]
        s = sin[...]
        turn = jnp.transpose(kv[:, :kvd])
        pieces = []
        for h in range(kv_heads):
            a = turn[h * hd:h * hd + half]
            d = turn[h * hd + half:(h + 1) * hd]
            pieces += [a * c + d * s, d * c - a * s]
        dkb = jnp.transpose(jnp.concatenate(pieces, axis=0)).astype(bf16)
        dvb = kv[:, kvd:].astype(bf16)
        pg = jnp.concatenate([dqr[...], dkb, dvb], axis=1)
        ing = nt(pg, w[:, :qkv])
        xf = x[...].astype(f32)
        scale = lax.rsqrt(jnp.mean(xf * xf, axis=-1, keepdims=True) + epsilon)
        plain = xf * scale
        ag = jnp.sum(ing * plain, axis=0, keepdims=True)
        e = ing * gain[0:1]
        grad_out[...] = mgr[...] + scale * (e - plain * jnp.mean(e * plain, axis=-1, keepdims=True))
        g[:, :2 * kvd] = nn(nbt[...], pg[:, qd:])
        sub = lax.broadcasted_iota(jnp.int32, (128, width), 0)
        both = jnp.where(sub == 0, ag, jnp.where(sub == 1, fgr[0:1], 0.0))
        g[:, 2 * kvd:] = jnp.transpose(both)
        split_rows(g, keep, give, ids_ref)

    small = sds((nf, nz, dr, 2 * kvd + 128), f32)
    input_grad, keep, give = call(
        last_kernel, ids, [kv_recv, dq, x_in, nb_t, gains, fg, mid_grad, attn_own, attn_oth, cos_t, sin_t],
        [sds((rows, width), f32), small, small],
        scratch=[sds((width, cols), bf16), sds((width, 2 * kvd + 128), f32)],
        flops=2 * rows * width * (qkv + 2 * kvd), name="last")
    rest = reduce_all(keep, give, "rest")

    dn_mine, dn_others = add_split(dn_keep, swap(dn_give), bf16, "down_c")
    w_down_grad = merge(dn_mine, [send_z(dn_others[d - 1], d) for d in range(1, nz)], "down_z")

    in_mine, in_others = add_split(in_keep, swap(in_give), bf16, "in_c")
    in_recv = [send_z(in_others[d - 1], d) for d in range(1, nz)]

    def in_split_kernel(ids_ref, mine, recv, outs, s):
        t = mine[...]
        for r in recv:
            t = t + r[...].astype(f32)
        s[...] = t
        for d in range(nf):
            outs[d][...] = s[pl.ds(pl.multiple_of((ids_ref[2] ^ d) * dr, 8), dr), :]

    (in_rows,) = call(in_split_kernel, ids, [in_mine, in_recv], [[sds((dr, 2 * hid), f32)] * nf],
                      scratch=[sds((blk, 2 * hid), f32)], name="in_z")
    in_pieces = [in_rows[0]] + [send_f(in_rows[d], d) for d in range(1, nf)]

    def unpack_kernel(ids_ref, p, g_out, u_out, s):
        for d in range(nf):
            s[ids_ref[2] ^ d] = p[d][...]
        for j in range(nf):
            for c in range(nc):
                at = (c * nf + j) * fr
                for w, a, b in ((g_out, c * frm, 2 * main + c * frt), (u_out, main + c * frm, 2 * main + tail + c * frt)):
                    w[:, at:at + frm] = s[j, :, a:a + frm]
                    if frt:
                        w[:, at + frm:at + fr] = s[j, :, b:b + frt]

    w_gate_grad, w_up_grad = call(
        unpack_kernel, ids, [in_pieces], [sds(w_gate.shape, f32), sds(w_up.shape, f32)],
        scratch=[sds((nf, dr, 2 * hid), f32)], name="unpack")

    return (
        block_out[None],
        input_grad[None],
        rest[:, 2 * kvd],
        w_query_grad,
        rest[:, :kvd],
        rest[:, kvd:2 * kvd],
        w_out_grad,
        rest[:, 2 * kvd + 1],
        w_gate_grad,
        w_up_grad,
        w_down_grad,
    )


def make_body(nc, nf):
    general = general_body(nc, nf)

    def body(*args):
        rows = args[0].shape[1]
        if tiled_fits(nc, nf, args[3].shape[0], args[10].shape[0], rows, args[4].shape[1]):
            return tiled_body(nc, nf, args)
        return general(*args)

    return body


def solution(mesh):
    tokens = P("fsdp", "ctx", None)
    shard = P(("ctx", "fsdp"))
    shard2 = P(("ctx", "fsdp"), None)
    return jax.shard_map(
        make_body(mesh.shape["ctx"], mesh.shape["fsdp"]),
        mesh=mesh,
        in_specs=(tokens, P("fsdp", "ctx"), shard, shard2, shard2, shard2, shard2, shard,
                  shard2, shard2, shard2, tokens),
        out_specs=(tokens, tokens, shard, shard2, shard2, shard2, shard2, shard,
                   shard2, shard2, shard2),
        check_vma=False,
    )
```

```python
import jax
import jax.numpy as jnp
from jax import lax
from jax.experimental import pallas as pl
from jax.experimental.pallas import tpu as pltpu
from jax.sharding import PartitionSpec as P


HEAD_DIM = 64

epsilon = 1e-05
rope_base = 10000.0
masked_score = -1e30
bf16 = jnp.bfloat16
f32 = jnp.float32


def dot32(left, right):
    return jnp.dot(left, right, preferred_element_type=f32)


def dot_t(left, right):
    return lax.dot_general(left, right, (((1,), (1,)), ((), ())), preferred_element_type=f32)


def t_dot(left, right):
    return lax.dot_general(left, right, (((0,), (0,)), ((), ())), preferred_element_type=f32)


def rope_tables(position):
    half_dim = HEAD_DIM // 2
    steps_f = jnp.arange(half_dim, dtype=f32)
    frequency = jnp.exp(steps_f * (-2.0 * jnp.log(f32(rope_base)) / HEAD_DIM))
    angles = position.astype(f32)[:, None] * frequency[None, :]
    cosine = jnp.concatenate([jnp.cos(angles), jnp.cos(angles)], axis=1)
    sine = jnp.concatenate([jnp.sin(angles), jnp.sin(angles)], axis=1)
    return (cosine, sine)


def rotate(values, cosine, sine):
    half_dim = values.shape[-1] // 2
    turned = jnp.concatenate([-values[..., half_dim:], values[..., :half_dim]], axis=-1)
    return values * cosine[:, None, :] + turned * sine[:, None, :]


def rotate_back(grad_in, cosine, sine):
    half_dim = grad_in.shape[-1] // 2
    shifted = grad_in * sine[:, None, :]
    turned = jnp.concatenate([shifted[..., half_dim:], -shifted[..., :half_dim]], axis=-1)
    return grad_in * cosine[:, None, :] + turned


def normalize(values, gain):
    norm_scale = lax.rsqrt(jnp.mean(values * values, axis=-1, keepdims=True) + epsilon)
    plain = values * norm_scale
    return (plain, norm_scale, plain * gain.astype(f32)[None, :])


def norm_back(d_out, plain, norm_scale, gain):
    gain_grad = jnp.sum(d_out * plain, axis=0)
    scaled = d_out * gain.astype(f32)[None, :]
    d_in = norm_scale * (scaled - plain * jnp.mean(scaled * plain, axis=-1, keepdims=True))
    return (d_in, gain_grad)


def general_body(nc, nf):
    nz = nc // 2
    power = nz & (nz - 1) == 0
    fpower = nf & (nf - 1) == 0
    swap_pairs = [(i, i ^ 1) for i in range(nc)]
    z_groups = [[2 * z + k for z in range(nz)] for k in range(2)]

    def step_to(at, d, n, pow2):
        return at ^ d if pow2 else (at + d) % n

    def step_from(at, d, n, pow2):
        return at ^ d if pow2 else (at + n - d) % n

    def swap(x):
        return lax.ppermute(x, "ctx", swap_pairs)

    def send_z(x, d):
        pairs = [(2 * z + k, 2 * step_to(z, d, nz, power) + k) for z in range(nz) for k in range(2)]
        return lax.ppermute(x, "ctx", pairs)

    def send_f(x, d):
        return lax.ppermute(x, "fsdp", [(i, step_to(i, d, nf, fpower)) for i in range(nf)])

    def gather_z(x, z):
        out = jnp.zeros((nz,) + x.shape, x.dtype)
        out = lax.dynamic_update_index_in_dim(out, x, z, 0)
        for d in range(1, nz):
            out = lax.dynamic_update_index_in_dim(out, send_z(x, d), step_from(z, d, nz, power), 0)
        return out

    def gather_f(x, f):
        out = jnp.zeros((nf,) + x.shape, x.dtype)
        out = lax.dynamic_update_index_in_dim(out, x, f, 0)
        for d in range(1, nf):
            out = lax.dynamic_update_index_in_dim(out, send_f(x, d), step_from(f, d, nf, fpower), 0)
        return out

    def scatter_z(x, z):
        total = lax.dynamic_index_in_dim(x, z, 0, keepdims=False)
        for d in range(1, nz):
            piece = lax.dynamic_index_in_dim(x, step_to(z, d, nz, power), 0, keepdims=False)
            total = total + send_z(piece.astype(bf16), d).astype(f32)
        return total

    def scatter_f(x, f):
        total = lax.dynamic_index_in_dim(x, f, 0, keepdims=False)
        for d in range(1, nf):
            piece = lax.dynamic_index_in_dim(x, step_to(f, d, nf, fpower), 0, keepdims=False)
            total = total + send_f(piece.astype(bf16), d).astype(f32)
        return total

    def a2a_f(x):
        return lax.all_to_all(x, "fsdp", 0, 0, tiled=True)

    def a2a_z(x):
        return lax.all_to_all(x, "ctx", 0, 0, tiled=True, axis_index_groups=z_groups)

    def spread(x, n):
        return jnp.broadcast_to(x[None], (n,) + x.shape)

    def both_cores(own, k, axis):
        other = swap(own)
        first = jnp.where(k == 0, own, other)
        second = jnp.where(k == 0, other, own)
        return jnp.stack([first, second], axis=axis)

    def core_sum(x, k, dtype):
        keep = jnp.where(k == 0, x[:, 0], x[:, 1])
        give = jnp.where(k == 0, x[:, 1], x[:, 0])
        return keep + swap(give.astype(dtype)).astype(f32)

    def body(
        hidden_in,
        positions,
        attn_gain,
        w_query,
        w_key,
        w_value,
        w_out,
        ffn_gain,
        w_gate,
        w_up,
        w_down,
        cotangent,
    ):
        x_in = hidden_in[0]
        local_pos = positions[0]
        cot = cotangent[0]
        rows, width = x_in.shape
        dr = w_query.shape[0]
        kvd = w_key.shape[1]
        heads = w_query.shape[1] // HEAD_DIM
        kv_heads = kvd // HEAD_DIM
        group = heads // kv_heads
        factor = HEAD_DIM ** (-0.5)
        qkv = w_query.shape[1] + 2 * kvd
        fr = w_down.shape[0]
        hid = nc * fr
        main = hid // 128 * 128
        tail = hid - main
        ctx = lax.axis_index("ctx")
        f = lax.axis_index("fsdp")
        z = ctx // 2
        k = ctx % 2

        w_attn = jnp.concatenate([w_query, w_key, w_value], axis=1)
        attn_z = gather_z(w_attn, z)
        gains = lax.all_to_all(
            jnp.broadcast_to(jnp.concatenate([attn_gain, ffn_gain])[None], (nc * nf, 2 * dr)),
            ("ctx", "fsdp"), 0, 0, tiled=True)
        gain_a = gains[:, :dr].reshape(width)
        gain_f = gains[:, dr:].reshape(width)
        attn_f = a2a_f(spread(attn_z, nf))
        attn_full = both_cores(attn_f, k, 0).transpose(2, 0, 1, 3, 4).reshape(width, qkv)

        def columns(w):
            return w.reshape(dr, nc, nf, fr).transpose(2, 0, 1, 3).reshape(nf, dr, hid)

        def packed(a, b):
            return jnp.concatenate([a[..., :main], b[..., :main], a[..., main:], b[..., main:]], axis=-1)

        def unpacked(p):
            return (
                jnp.concatenate([p[..., :main], p[..., 2 * main:2 * main + tail]], axis=-1),
                jnp.concatenate([p[..., main:2 * main], p[..., 2 * main + tail:]], axis=-1),
            )

        w_in = a2a_f(packed(columns(w_gate), columns(w_up))).reshape(nf * dr, 2 * hid)

        resid_in = x_in.astype(f32)
        plain_a, scale_a, normed_a = normalize(resid_in, gain_a)
        normed_b = normed_a.astype(bf16)
        cosine, sine = rope_tables(local_pos)
        proj = dot32(normed_b, attn_full)
        queries = rotate(proj[:, :width].reshape(rows, heads, HEAD_DIM), cosine, sine).astype(bf16)
        q_heads = queries.reshape(rows, kv_heads, group, HEAD_DIM)
        keys_local = (
            rotate(proj[:, width:width + kvd].reshape(rows, kv_heads, HEAD_DIM), cosine, sine)
            .astype(bf16)
            .reshape(rows, kvd)
        )
        values_local = proj[:, width + kvd:].astype(bf16)

        high = (local_pos // 64).astype(bf16)
        low = (local_pos % 64).astype(bf16)
        extra = jnp.pad(jnp.stack([high, low]), ((0, 14), (0, 2 * kvd - rows)))
        kv_own = jnp.concatenate([jnp.concatenate([keys_local, values_local], axis=1), extra], axis=0)
        kv_z = a2a_z(spread(kv_own, nz))
        kv_all = jnp.stack([kv_z, swap(kv_z)])
        length = nc * rows
        keys_all = kv_all[:, :, :rows, :kvd].reshape(length, kv_heads, HEAD_DIM)
        values_all = kv_all[:, :, :rows, kvd:].reshape(length, kv_heads, HEAD_DIM)
        key_pos = (kv_all[:, :, rows, :rows].astype(f32) * 64.0 + kv_all[:, :, rows + 1, :rows].astype(f32)).reshape(length)

        w_in_z = gather_z(w_in, z)
        w_down_z = gather_z(w_down, z)
        w_out_z = gather_z(w_out, z)
        cot_g = gather_f(cot, f).reshape(nf * rows, width)
        w_out_f = gather_f(w_out_z, f)
        out_full = both_cores(w_out_f, k, 0).transpose(2, 0, 1, 3, 4).reshape(width, width)
        w_in_full = both_cores(w_in_z, k, 1).reshape(width, 2 * hid)
        w_down_full = both_cores(w_down_z, k, 1).reshape(hid, width)

        allowed = (key_pos[None, :] <= local_pos.astype(f32)[:, None])[None, None]

        def scores_of(q, keys):
            s = jnp.einsum("qkgd,lkd->kgql", q, keys, preferred_element_type=f32) * factor
            return jnp.where(allowed, s, masked_score)

        scores = scores_of(q_heads, keys_all)
        highest = jnp.max(scores, axis=-1, keepdims=True)
        summed = jnp.sum(jnp.where(allowed, jnp.exp(scores - highest), 0.0), axis=-1, keepdims=True)
        log_total = highest + jnp.log(summed)
        probs = jnp.where(allowed, jnp.exp(scores - log_total), 0.0).astype(bf16)
        attn_heads = jnp.einsum("kgql,lkd->qkgd", probs, values_all, preferred_element_type=f32).astype(bf16)
        attn_flat = attn_heads.reshape(rows, width)
        resid_mid = resid_in + dot32(attn_flat, out_full)
        plain_f, scale_f, normed_f = normalize(resid_mid, gain_f)
        normed_h = a2a_f(spread(normed_f.astype(bf16), nf)).reshape(nf * rows, width)

        gate, up = unpacked(dot32(normed_h, w_in_full))
        sig = jax.nn.sigmoid(gate)
        silu = gate * sig
        activation = (silu * up).astype(bf16)
        act_grad = dot_t(cot_g, w_down_full)
        up_grad = (act_grad * silu).astype(bf16)
        gate_grad = (act_grad * up * sig * (1.0 + gate * (1.0 - sig))).astype(bf16)
        in_grad = packed(gate_grad, up_grad)
        normed_part = dot_t(in_grad, w_in_full)
        normed_grad = jnp.sum(a2a_f(normed_part.reshape(nf, rows, width)), axis=0)

        block_part = dot32(activation, w_down_full).reshape(nf, rows, width)
        block_out = resid_mid + scatter_f(block_part, f)

        w_in_part = t_dot(normed_h, in_grad).reshape(nz, 2, nf * dr, 2 * hid)
        w_down_part = t_dot(activation, cot_g).reshape(nz, 2, fr, width)
        w_in_sum = scatter_z(core_sum(w_in_part, k, f32), z)
        w_down_grad = scatter_z(core_sum(w_down_part, k, f32), z)

        mid_norm_grad, ffn_gain_grad = norm_back(normed_grad, plain_f, scale_f, gain_f)
        mid_grad = cot.astype(f32) + mid_norm_grad
        mid_grad_b = mid_grad.astype(bf16)
        attn_grad = dot_t(mid_grad_b, out_full).astype(bf16).reshape(rows, kv_heads, group, HEAD_DIM)
        delta = jnp.einsum("qkgd,qkgd->kgq", attn_grad, attn_heads, preferred_element_type=f32)

        scores2 = scores_of(q_heads, keys_all)
        probs_f = jnp.where(allowed, jnp.exp(scores2 - log_total), 0.0)
        value_grad = jnp.einsum("kgql,qkgd->lkd", probs_f.astype(bf16), attn_grad, preferred_element_type=f32)
        d_probs = jnp.einsum("qkgd,lkd->kgql", attn_grad, values_all, preferred_element_type=f32)
        d_scores = (probs_f * (d_probs - delta[..., None]) * factor).astype(bf16)
        query_grad = jnp.einsum("kgql,lkd->qkgd", d_scores, keys_all, preferred_element_type=f32)
        key_grad = jnp.einsum("kgql,qkgd->lkd", d_scores, q_heads, preferred_element_type=f32)
        kv_part = jnp.concatenate([key_grad.reshape(length, kvd), value_grad.reshape(length, kvd)], axis=1)
        kv_part = kv_part.reshape(2, nz, rows, 2 * kvd)
        kv_sum = kv_part[0] + swap(kv_part[1])
        kv_grad = jnp.sum(a2a_z(kv_sum), axis=0)

        query_grad_b = (
            rotate_back(query_grad.reshape(rows, heads, HEAD_DIM), cosine, sine)
            .astype(bf16)
            .reshape(rows, width)
        )
        key_grad_b = (
            rotate_back(kv_grad[:, :kvd].reshape(rows, kv_heads, HEAD_DIM), cosine, sine)
            .astype(bf16)
            .reshape(rows, kvd)
        )
        value_grad_b = kv_grad[:, kvd:].astype(bf16)
        proj_grad = jnp.concatenate([query_grad_b, key_grad_b, value_grad_b], axis=1)
        input_norm_grad = dot_t(proj_grad, attn_full)
        in_norm_grad, attn_gain_grad = norm_back(input_norm_grad, plain_a, scale_a, gain_a)
        input_grad = mid_grad + in_norm_grad

        def reduce_all(part, cols):
            part = part.reshape(nz, 2, nf, dr, cols).transpose(2, 1, 0, 3, 4)
            part = core_sum(part, k, f32)
            part = scatter_f(part, f)
            return scatter_z(part, z)

        w_out_grad = reduce_all(t_dot(attn_flat, mid_grad_b), width)
        w_attn_grad = reduce_all(t_dot(normed_b, proj_grad), qkv)

        gain_parts = jnp.concatenate(
            [attn_gain_grad.reshape(nc * nf, dr), ffn_gain_grad.reshape(nc * nf, dr)], axis=1)
        gain_grads = jnp.sum(
            lax.all_to_all(gain_parts, ("ctx", "fsdp"), 0, 0, tiled=True), axis=0)

        w_in_rows = a2a_f(w_in_sum.reshape(nf, dr, 2 * hid))

        def owner_columns(p):
            return p.reshape(nf, dr, nc, fr).transpose(1, 2, 0, 3).reshape(dr, nc * nf * fr)

        gate_cols, up_cols = unpacked(w_in_rows)
        return (
            block_out[None],
            input_grad[None],
            gain_grads[:dr],
            w_attn_grad[:, :width],
            w_attn_grad[:, width:width + kvd],
            w_attn_grad[:, width + kvd:],
            w_out_grad,
            gain_grads[dr:],
            owner_columns(gate_cols),
            owner_columns(up_cols),
            w_down_grad,
        )

    return body


VMEM = pl.BlockSpec(memory_space=pltpu.VMEM)
SMEM = pl.BlockSpec(memory_space=pltpu.SMEM)


def sds(shape, dtype):
    return jax.ShapeDtypeStruct(shape, dtype)


def size_of(x):
    return x.size * jnp.dtype(x.dtype).itemsize


def call(kernel, ids, ins, outs, scratch=(), flops=0, fetch=False):
    flat_in, in_tree = jax.tree.flatten(ins)
    flat_out, out_tree = jax.tree.flatten(outs)
    n, m, k = len(flat_in), len(flat_out), len(scratch)
    moved = sum(size_of(x) for x in flat_in + flat_out)
    held = sum(size_of(x) for x in scratch)

    def run(ids_ref, *refs):
        given, made, work = refs[:n], refs[n:n + m], refs[n + m:n + m + k]
        if fetch:
            local, sems = refs[n + m + k:-1], refs[-1]
            copies = [pltpu.make_async_copy(a, b, sems.at[i]) for i, (a, b) in enumerate(zip(given, local))]
            for c in copies:
                c.start()
            for c in copies:
                c.wait()
            given = local
        kernel(ids_ref, *jax.tree.unflatten(in_tree, given), *jax.tree.unflatten(out_tree, made), *work)

    spaces = [pl.BlockSpec(memory_space=pltpu.HBM)] * n if fetch else [VMEM] * n
    extra = [pltpu.VMEM(x.shape, x.dtype) for x in flat_in] + [pltpu.SemaphoreType.DMA((n,))] if fetch else []
    kernel_call = pl.pallas_call(
        run,
        out_shape=tuple(flat_out),
        in_specs=[SMEM] + spaces,
        out_specs=tuple([VMEM] * m),
        scratch_shapes=[pltpu.VMEM(x.shape, x.dtype) for x in scratch] + extra,
        compiler_params=pltpu.CompilerParams(vmem_limit_bytes=min(60 << 20, moved + held + (16 << 20))),
        cost_estimate=pl.CostEstimate(flops=int(flops), transcendentals=0, bytes_accessed=int(moved)),
    )
    got = kernel_call(ids, *[pltpu.with_memory_space_constraint(x, pltpu.HBM) if fetch else x for x in flat_in])
    return jax.tree.unflatten(out_tree, got)


def nn(a, b):
    return lax.dot_general(a, b, (((1,), (0,)), ((), ())), preferred_element_type=f32)


def nt(a, b):
    return lax.dot_general(a, b, (((1,), (1,)), ((), ())), preferred_element_type=f32)


def tn(a, b):
    return lax.dot_general(a, b, (((0,), (0,)), ((), ())), preferred_element_type=f32)


def coded(n, c):
    tiles = c // 128
    return sds((n * tiles + (tiles + 15) // 16 * 16, 128), jnp.int16)


def encode(v, put):
    n, c = v.shape
    exps = []
    for t in range(c // 128):
        x = v[:, t * 128:(t + 1) * 128]
        top = jnp.max(jnp.abs(x), axis=0, keepdims=True)
        e = jnp.clip(jnp.ceil(jnp.log2(jnp.maximum(top, 1e-37))), -110.0, 120.0)
        q = jnp.clip(jnp.round(x * (32000.0 * jnp.exp2(-e))), -32767.0, 32767.0)
        put(slice(t * n, (t + 1) * n), q.astype(jnp.int32).astype(jnp.int16))
        exps.append(e)
    spare = -len(exps) % 16
    if spare:
        exps.append(jnp.zeros((spare, 128), f32))
    put(slice(n * (c // 128), None), jnp.concatenate(exps, axis=0).astype(jnp.int32).astype(jnp.int16))


def encode_to(ref, v, *lead):
    def put(rows, q):
        ref[(*lead, rows, slice(None))] = q

    encode(v, put)


def decode(p, n, c):
    tiles = c // 128
    exps = jnp.exp2(p[n * tiles:, :].astype(jnp.int32).astype(f32)) * (1.0 / 32000.0)
    return jnp.concatenate(
        [p[t * n:(t + 1) * n, :].astype(jnp.int32).astype(f32) * exps[t:t + 1] for t in range(tiles)], axis=1)


class Chunk:
    def __init__(self, nc, off, fr, width):
        self.off, self.fr = off, fr
        self.frm = fr // 16 * 16
        self.frt = fr - self.frm
        self.main = nc * self.frm
        self.tail = nc * self.frt
        self.hid = self.main + self.tail
        self.wide = 2 * self.hid
        self.rows = fr * width // self.wide

    def fits(self, width):
        return (
            self.fr % 8 == 0 and self.main % 128 == 0 and (2 * self.tail) % 128 == 0 and self.wide % 128 == 0
            and self.wide < width and width % 128 == 0
            and self.rows * self.wide == self.fr * width and self.rows % 16 == 0 and (self.rows - self.fr) % 8 == 0
        )

    def fold(self, v):
        width, wide, more = v.shape[1], self.wide, self.rows - self.fr
        low = jnp.concatenate([v[:, t:t + 128] for t in range(wide, width, 128)], axis=0)
        low = jnp.concatenate([low[t * more:(t + 1) * more] for t in range(wide // 128)], axis=1)
        return jnp.concatenate([v[:, :wide], low], axis=0)

    def unfold(self, v, width):
        fr = self.fr
        low = jnp.concatenate([v[fr:, t:t + 128] for t in range(0, self.wide, 128)], axis=0)
        low = jnp.concatenate([low[t * fr:(t + 1) * fr] for t in range((width - self.wide) // 128)], axis=1)
        return jnp.concatenate([v[:fr], low], axis=1)


def chunks_of(nc, fr, width):
    first = (fr // 2 + 15) // 16 * 16
    return [Chunk(nc, 0, first, width), Chunk(nc, first, fr - first, width)]


def tiled_fits(nc, nf, dr, fr, rows, kvd, width):
    nz = nc // 2
    return (
        nz & (nz - 1) == 0 and nf & (nf - 1) == 0
        and dr % 16 == 0 and rows == 128 and kvd == 128
        and all(c.fr > 0 and c.fits(width) for c in chunks_of(nc, fr, width))
    )


def tiled_body(nc, nf, args):
    nz = nc // 2

    def swap(x):
        return lax.ppermute(x, "ctx", [(i, i ^ 1) for i in range(nc)])

    def send_z(x, d):
        return lax.ppermute(x, "ctx", [(i, i ^ (2 * d)) for i in range(nc)])

    def send_f(x, d):
        return lax.ppermute(x, "fsdp", [(i, i ^ d) for i in range(nf)])

    def gather_z(x):
        return [x] + [send_z(x, d) for d in range(1, nz)]

    def gather_f(x):
        return [x] + [send_f(x, d) for d in range(1, nf)]

    (hidden_in, positions, attn_gain, w_query, w_key, w_value, w_out, ffn_gain,
     w_gate, w_up, w_down, cotangent) = args
    x_in = hidden_in[0]
    cot = cotangent[0]
    rows, width = x_in.shape
    dr = w_query.shape[0]
    kvd = w_key.shape[1]
    qd = w_query.shape[1]
    hd = HEAD_DIM
    half = hd // 2
    heads = qd // hd
    kv_heads = kvd // hd
    group = heads // kv_heads
    factor = hd ** (-0.5)
    qkv = qd + 2 * kvd
    cols = qkv + 128
    length = nc * rows
    blk = nf * dr
    fr = w_down.shape[0]
    chunks = chunks_of(nc, fr, width)
    bases = [0, chunks[0].wide]
    wide_all = sum(c.wide for c in chunks)
    xrows = 16
    ctx = lax.axis_index("ctx")
    ids = jnp.stack([ctx % 2, ctx // 2, lax.axis_index("fsdp")]).astype(jnp.int32)

    def stacked(n, r, c):
        one = coded(r, c)
        return sds((n,) + one.shape, one.dtype)

    def assemble(dst, own, oth, ids_ref):
        k, z0, f0 = ids_ref[0], ids_ref[1], ids_ref[2]
        for src, side in ((own, k), (oth, 1 - k)):
            for d in range(nf):
                for e in range(nz):
                    at = ((z0 ^ e) * 2 + side) * blk + (f0 ^ d) * dr
                    dst[pl.ds(pl.multiple_of(at, 16), dr), :] = src[d][e]

    def column(row):
        n = row.shape[1]
        a = lax.broadcasted_iota(jnp.int32, (n, n), 0)
        b = lax.broadcasted_iota(jnp.int32, (n, n), 1)
        return jnp.sum(jnp.where(a == b, jnp.broadcast_to(row, (n, n)), 0.0), axis=1, keepdims=True)

    def stack_kernel(ids_ref, pieces, out):
        for d, p in enumerate(pieces):
            out[d] = p[...]

    def stack(pieces):
        return call(stack_kernel, ids, [pieces], [sds((len(pieces),) + pieces[0].shape, pieces[0].dtype)])[0]

    def pack_kernel(ids_ref, wq, wk, wv, gg, wa):
        lane = lax.broadcasted_iota(jnp.int32, (dr, 128), 1)
        a = column(gg[0:1])
        b = column(gg[1:2])
        wa[:, :qd] = wq[...]
        wa[:, qd:qd + kvd] = wk[...]
        wa[:, qd + kvd:qkv] = wv[...]
        wa[:, qkv:] = jnp.where(lane == 0, a, jnp.where(lane == 1, b, 0.0)).astype(bf16)

    (wa,) = call(pack_kernel, ids, [w_query, w_key, w_value, jnp.stack([attn_gain, ffn_gain]).astype(f32)],
                 [sds((dr, cols), bf16)], fetch=True)
    attn_own = gather_f(stack(gather_z(wa)))
    attn_oth = [swap(p) for p in attn_own]

    def columns(g_ref, u_ref):
        for j in range(nf):
            for ch, base in zip(chunks, bases):
                for c in range(nc):
                    at = (c * nf + j) * fr + ch.off
                    for w, a, b in (
                        (g_ref, base + c * ch.frm, base + 2 * ch.main + c * ch.frt),
                        (u_ref, base + ch.main + c * ch.frm, base + 2 * ch.main + ch.tail + c * ch.frt),
                    ):
                        yield w, j, at, a, ch.frm
                        if ch.frt:
                            yield w, j, at + ch.frm, b, ch.frt

    def pack_in_kernel(ids_ref, wg, wu, wdn, wi, wdp, s):
        for ch, out in zip(chunks, wdp):
            out[...] = ch.fold(wdn[ch.off:ch.off + ch.fr, :].astype(f32)).astype(bf16)
        for w, j, at, to, n in columns(wg, wu):
            s[j, :, to:to + n] = w[:, at:at + n]
        for d in range(nf):
            wi[d][...] = s[ids_ref[2] ^ d]

    wi, wdp = call(pack_in_kernel, ids, [w_gate, w_up, w_down],
                   [[sds((dr, wide_all), bf16)] * nf, [sds((ch.rows, ch.wide), bf16) for ch in chunks]],
                   scratch=[sds((nf, dr, wide_all), bf16)], fetch=True)

    pos_row = positions.astype(f32)
    steps_f = jnp.arange(half, dtype=f32)
    frequency = jnp.exp(steps_f * (-2.0 * jnp.log(f32(rope_base)) / hd))
    angles = frequency[:, None] * pos_row
    cos_t = jnp.cos(angles)
    sin_t = jnp.sin(angles)
    extra = jnp.pad(
        jnp.concatenate([positions // 64, positions % 64], axis=0).astype(bf16),
        ((0, xrows - 2), (0, 2 * kvd - rows)))

    def proj_kernel(ids_ref, x, own, oth, cos, sin, ext, q_out, kv_out, gain_out, nb_out, w):
        assemble(w, own, oth, ids_ref)
        gains = jnp.transpose(w[:, qkv:].astype(f32))
        gain_out[...] = gains[0:8]
        xf = x[...].astype(f32)
        scale = lax.rsqrt(jnp.mean(xf * xf, axis=-1, keepdims=True) + epsilon)
        normed = xf * scale * gains[0:1]
        nb = normed.astype(bf16)
        nb_out[...] = jnp.transpose(nb.astype(f32)).astype(bf16)
        proj = nn(nb, w[:, :qkv])
        c = cos[...]
        s = sin[...]
        turn = jnp.transpose(proj[:, :qd + kvd])
        for h in range(heads):
            a = turn[h * hd:h * hd + half]
            b = turn[h * hd + half:(h + 1) * hd]
            q_out[h * hd:h * hd + half] = (a * c - b * s).astype(bf16)
            q_out[h * hd + half:(h + 1) * hd] = (b * c + a * s).astype(bf16)
        parts = []
        for h in range(kv_heads):
            a = turn[qd + h * hd:qd + h * hd + half]
            b = turn[qd + h * hd + half:qd + (h + 1) * hd]
            parts += [a * c - b * s, b * c + a * s]
        kv_out[:rows, :kvd] = jnp.transpose(jnp.concatenate(parts, axis=0)).astype(bf16)
        kv_out[:rows, kvd:] = proj[:, qd + kvd:].astype(bf16)
        kv_out[rows:, :] = ext[...]

    q_t, kv_mine, gains, nb_t = call(
        proj_kernel, ids, [x_in, attn_own, attn_oth, cos_t, sin_t, extra],
        [sds((qd, rows), bf16), sds((rows + xrows, 2 * kvd), bf16), sds((8, width), f32), sds((width, rows), bf16)],
        scratch=[sds((width, cols), bf16)], flops=2 * rows * width * qkv)

    kv_own = gather_z(kv_mine)
    kv_oth = [swap(p) for p in kv_own]

    w_out_z = stack(gather_z(w_out))
    out_own = stack(gather_f(w_out_z))
    cot_all = gather_f(cot)
    out_oth = swap(out_own)

    def join_kernel(ids_ref, pieces, folded, outs):
        for ch, base, extra_r, out in zip(chunks, bases, folded, outs):
            for d in range(nf):
                out[d * dr:(d + 1) * dr, :] = pieces[d][:, base:base + ch.wide]
            out[blk:, :] = extra_r[...]

    (w_in,) = call(join_kernel, ids, [[wi[0]] + [send_f(wi[d], d) for d in range(1, nf)], wdp],
                   [[sds((blk + ch.rows, ch.wide), bf16) for ch in chunks]])
    w_in_own = [stack(gather_z(w)) for w in w_in]
    w_in_oth = [swap(w) for w in w_in_own]

    def load_keys(own, oth, pos, keys, bias):
        for i in range(nc):
            kv = own[i] if i < nz else oth[i - nz]
            keys[i * rows:(i + 1) * rows, :] = kv[:rows, :]
            ext = jnp.transpose(kv[rows:, :rows].astype(f32))
            kpos = ext[:, 0:1] * 64.0 + ext[:, 1:2]
            bias[i * rows:(i + 1) * rows, :] = jnp.where(kpos <= pos[...], 0.0, masked_score)

    def pair_of(ref, n):
        v = ref[pl.ds(pl.multiple_of(n * 2 * hd, 128), 2 * hd), :]
        return jnp.concatenate([v[:hd], v[hd:]], axis=1)

    def put_pair(ref, n, v):
        ref[pl.ds(pl.multiple_of(n * 2 * hd, 128), 2 * hd), :] = jnp.concatenate([v[:, :rows], v[:, rows:]], axis=0)

    pairs = group // 2

    def attn_kernel(ids_ref, q, kown, koth, pos, attn_out, lse_out, keys, bias, k_s, v_s):
        load_keys(kown, koth, pos, keys, bias)
        b = bias[...]
        bias2 = jnp.concatenate([b, b], axis=1)
        vals_t = jnp.transpose(keys[:, kvd:].astype(f32)).astype(bf16)
        for j in range(kv_heads):
            k_s[j] = keys[:, j * hd:(j + 1) * hd]
            v_s[j] = vals_t[j * hd:(j + 1) * hd]

        def one_head(j, carry):
            kj = k_s[j]
            vj = v_s[j]
            for i in range(pairs):
                n = j * pairs + i
                s = nn(kj, pair_of(q, n)) * factor + bias2
                high = jnp.max(s, axis=0, keepdims=True)
                e = jnp.exp(s - high)
                total = jnp.sum(e, axis=0, keepdims=True)
                p = (e * (1.0 / total)).astype(bf16)
                put_pair(attn_out, n, nn(vj, p).astype(bf16))
                lse_out[n] = high + jnp.log(total)
            return carry

        lax.fori_loop(0, kv_heads, one_head, 0)

    attn_t, lse = call(
        attn_kernel, ids, [q_t, kv_own, kv_oth, pos_row],
        [sds((qd, rows), bf16), sds((heads // 2, 1, 2 * rows), f32)],
        scratch=[sds((length, 2 * kvd), bf16), sds((length, rows), f32),
                 sds((kv_heads, length, hd), bf16), sds((kv_heads, hd, length), bf16)],
        flops=4 * heads * rows * length * 128)

    def outp_kernel(ids_ref, attn_r, x, own, oth, gain, mid_out, nf_out, w):
        assemble(w, own, oth, ids_ref)
        attn = jnp.transpose(attn_r[...].astype(f32)).astype(bf16)
        mid = x[...].astype(f32) + nn(attn, w[...])
        mid_out[...] = mid
        scale = lax.rsqrt(jnp.mean(mid * mid, axis=-1, keepdims=True) + epsilon)
        nf_out[...] = (mid * scale * gain[1:2]).astype(bf16)

    mid, nh_mine = call(
        outp_kernel, ids, [attn_t, x_in, out_own, out_oth, gains],
        [sds((rows, width), f32), sds((rows, width), bf16)],
        scratch=[sds((qd, width), bf16)], flops=2 * rows * qd * width)

    nh_all = gather_f(nh_mine)

    def weights_of(h):
        ch = chunks[h]

        def weights_kernel(ids_ref, iown, ioth, wi_out, wd_out):
            k, z0, f0 = ids_ref[0], ids_ref[1], ids_ref[2]
            for e in range(nz):
                for src, side in ((iown, k), (ioth, 1 - k)):
                    for d in range(nf):
                        at = ((z0 ^ e) * 2 + side) * blk + (f0 ^ d) * dr
                        wi_out[pl.ds(pl.multiple_of(at, 16), dr), :] = src[e, d * dr:(d + 1) * dr, :]
                mine = ch.unfold(iown[e, blk:, :].astype(f32), width)
                theirs = ch.unfold(ioth[e, blk:, :].astype(f32), width)
                for v, side in ((mine, k), (theirs, 1 - k)):
                    at = ((z0 ^ e) * 2 + side) * ch.frm
                    wd_out[pl.ds(pl.multiple_of(at, 16), ch.frm), :] = v[:ch.frm].astype(bf16)
                if ch.frt:
                    first = jnp.where(k == 0, mine[ch.frm:], theirs[ch.frm:])
                    second = jnp.where(k == 0, theirs[ch.frm:], mine[ch.frm:])
                    at = ch.main + (z0 ^ e) * 2 * ch.frt
                    wd_out[pl.ds(pl.multiple_of(at, 16), 2 * ch.frt), :] = jnp.concatenate(
                        [first, second], axis=0).astype(bf16)

        return call(weights_kernel, ids, [w_in_own[h], w_in_oth[h]],
                    [sds((width, ch.wide), bf16), sds((ch.hid, width), bf16)])

    w_pairs = [weights_of(h) for h in range(len(chunks))]

    def ffn_of(h, d, before):
        ch = chunks[h]
        main, tail = ch.main, ch.tail

        def ffn_kernel(ids_ref, nh, ct, wi_r, wd_r, prev, act_out, grad_out, part_out):
            g = nn(nh[...], wi_r[...])
            ag = nt(ct[...], wd_r[...])

            def one(gate, up, agn):
                sig = 1.0 / (1.0 + jnp.exp(-gate))
                silu = gate * sig
                return (
                    (silu * up).astype(bf16),
                    (agn * up * sig * (1.0 + gate * (1.0 - sig))).astype(bf16),
                    (agn * silu).astype(bf16),
                )

            a, gg, ug = one(g[:, :main], g[:, main:2 * main], ag[:, :main])
            act_out[:, :main] = a
            grad_out[:, :main] = gg
            grad_out[:, main:2 * main] = ug
            if tail:
                t = g[:, 2 * main:]
                a, gg, ug = one(t[:, :tail], t[:, tail:], ag[:, main:])
                act_out[:, main:] = a
                grad_out[:, 2 * main:] = jnp.concatenate([gg, ug], axis=1)
            part = nt(grad_out[...], wi_r[...])
            for p in prev:
                part = part + p[...]
            if len(prev) == len(chunks) - 1 and d > 0:
                encode_to(part_out, part)
            else:
                part_out[...] = part

        return call(
            ffn_kernel, ids, [nh_all[d], cot_all[d], w_pairs[h][0], w_pairs[h][1], before],
            [sds((rows, ch.hid), bf16), sds((rows, ch.wide), bf16),
             coded(rows, width) if len(before) == len(chunks) - 1 and d > 0 else sds((rows, width), f32)],
            flops=2 * rows * width * 5 * ch.hid)

    acts, in_grads = [], []
    parts = [None] * nf
    for h in range(len(chunks)):
        acts.append([])
        in_grads.append([])
        for d in range(nf):
            a, g, parts[d] = ffn_of(h, d, [] if parts[d] is None else [parts[d]])
            acts[h].append(a)
            in_grads[h].append(g)
    norm_recv = [parts[0]] + [send_f(parts[d], d) for d in range(1, nf)]

    def in_grad_of(h):
        ch = chunks[h]

        def in_grad_kernel(ids_ref, nh, gradr, ct, actr, keep, give, gi_s, gd_s):
            k, z0 = ids_ref[0], ids_ref[1]
            nh2 = jnp.concatenate([a[...] for a in nh], axis=0)
            gr2 = jnp.concatenate([a[...] for a in gradr], axis=0)
            gi_s[...] = tn(nh2, gr2)
            act = jnp.concatenate([a[...] for a in actr], axis=0)
            ct2 = jnp.concatenate([a[...] for a in ct], axis=0)
            gd_s[...] = tn(act, ct2)

            def one(e, carry):
                for is_keep, side in ((False, 1 - k), (True, k)):
                    at = (z0 ^ e) * 2 + side
                    top = gi_s[pl.ds(pl.multiple_of(at * blk, 8), blk), :]
                    v = gd_s[pl.ds(pl.multiple_of(at * ch.frm, 8), ch.frm), :]
                    if ch.frt:
                        t = gd_s[pl.ds(pl.multiple_of(ch.main + at * ch.frt, 8), ch.frt), :]
                        v = jnp.concatenate([v, t], axis=0)
                    v = jnp.concatenate([top, ch.fold(v)], axis=0)
                    if is_keep:
                        keep[e] = v
                    else:
                        encode_to(give, v, e)
                return carry

            lax.fori_loop(0, nz, one, 0)

        return call(
            in_grad_kernel, ids, [nh_all, in_grads[h], cot_all, acts[h]],
            [sds((nz, blk + ch.rows, ch.wide), f32), stacked(nz, blk + ch.rows, ch.wide)],
            scratch=[sds((width, ch.wide), f32), sds((ch.hid, width), f32)],
            flops=2 * nf * rows * width * 3 * ch.hid)

    in_pairs = [in_grad_of(h) for h in range(len(chunks))]

    def block_kernel(ids_ref, actr, wd_r, blk_out):
        out = None
        for a_r, w_r in zip(actr, wd_r):
            t = nn(jnp.concatenate([a[...] for a in a_r], axis=0), w_r[...])
            out = t if out is None else out + t
        blk_out[0][...] = out[:rows]
        for d in range(1, nf):
            blk_out[d][...] = out[d * rows:(d + 1) * rows].astype(bf16)

    (blk_own,) = call(
        block_kernel, ids, [acts, [w[1] for w in w_pairs]],
        [[sds((rows, width), f32)] + [sds((rows, width), bf16)] * (nf - 1)],
        flops=2 * nf * rows * width * sum(c.hid for c in chunks))

    blk_recv = [send_f(blk_own[d], d) for d in range(1, nf)]
    block_out = mid + blk_own[0]
    for p in blk_recv:
        block_out = block_out + p.astype(f32)

    def mid_kernel(ids_ref, npart, midr, ct, gain, own, oth, mg_out, mgb_out, do_out, fg_out, w):
        assemble(w, own, oth, ids_ref)
        m = midr[...]
        scale = lax.rsqrt(jnp.mean(m * m, axis=-1, keepdims=True) + epsilon)
        plain = m * scale
        ng = npart[0][...]
        for i in range(1, nf):
            ng = ng + decode(npart[i], rows, width)
        fg_out[...] = jnp.broadcast_to(jnp.sum(ng * plain, axis=0, keepdims=True), (8, width))
        e = ng * gain[1:2]
        mg = ct[...].astype(f32) + scale * (e - plain * jnp.mean(e * plain, axis=-1, keepdims=True))
        mg_out[...] = mg
        mgb = mg.astype(bf16)
        mgb_out[...] = mgb
        do_out[...] = jnp.transpose(nt(mgb, w[...]).astype(bf16).astype(f32)).astype(bf16)

    mid_grad, mgb, do_t, fg = call(
        mid_kernel, ids, [norm_recv, mid, cot, gains, out_own, out_oth],
        [sds((rows, width), f32), sds((rows, width), bf16), sds((qd, rows), bf16), sds((8, width), f32)],
        scratch=[sds((qd, width), bf16)], flops=2 * rows * qd * width)

    def back_kernel(ids_ref, do_t, q, kown, koth, pos, attn, lse_r, cos, sin,
                    dq_out, kv_keep, kv_give, keys, bias, dq_t, k_s, kt_s, v_s, dk_s, dv_s):
        load_keys(kown, koth, pos, keys, bias)
        b = bias[...]
        bias2 = jnp.concatenate([b, b], axis=1)
        keys_t = jnp.transpose(keys[:, :kvd].astype(f32)).astype(bf16)
        for j in range(kv_heads):
            k_s[j] = keys[:, j * hd:(j + 1) * hd]
            kt_s[j] = keys_t[j * hd:(j + 1) * hd]
            v_s[j] = keys[:, kvd + j * hd:kvd + (j + 1) * hd]

        def one_head(j, carry):
            kj = k_s[j]
            ktj = kt_s[j]
            vj = v_s[j]
            dk = None
            dv = None
            for i in range(pairs):
                n = j * pairs + i
                qp = pair_of(q, n)
                dop = pair_of(do_t, n)
                op = pair_of(attn, n)
                delta = jnp.sum(dop.astype(f32) * op.astype(f32), axis=0, keepdims=True)
                p = jnp.exp(nn(kj, qp) * factor + bias2 - lse_r[n])
                dp = nn(vj, dop)
                ds = (p * (dp - delta) * factor).astype(bf16)
                put_pair(dq_t, n, nn(ktj, ds))
                pk = nt(ds, qp)
                pv = nt(p.astype(bf16), dop)
                dk = pk if dk is None else dk + pk
                dv = pv if dv is None else dv + pv
            dk_s[j] = dk
            dv_s[j] = dv
            return carry

        lax.fori_loop(0, kv_heads, one_head, 0)

        def side(i):
            sl = slice(i * rows, (i + 1) * rows)
            return jnp.concatenate([r[j, sl, :] for r in (dk_s, dv_s) for j in range(kv_heads)], axis=1)

        for i in range(nz):
            encode_to(kv_give, side(nz + i), i)
            kv_keep[i] = side(i)
        c = cos[...]
        s = sin[...]
        for h in range(heads):
            a = dq_t[h * hd:h * hd + half, :]
            d = dq_t[h * hd + half:(h + 1) * hd, :]
            dq_t[h * hd:h * hd + half, :] = a * c + d * s
            dq_t[h * hd + half:(h + 1) * hd, :] = d * c - a * s
        dq_out[...] = jnp.transpose(dq_t[...]).astype(bf16)

    dq, kv_keep, kv_give = call(
        back_kernel, ids, [do_t, q_t, kv_own, kv_oth, pos_row, attn_t, lse, cos_t, sin_t],
        [sds((rows, qd), bf16), sds((nz, rows, 2 * kvd), f32), stacked(nz, rows, 2 * kvd)],
        scratch=[sds((length, 2 * kvd), bf16), sds((length, rows), f32), sds((qd, rows), f32),
                 sds((kv_heads, length, hd), bf16), sds((kv_heads, hd, length), bf16), sds((kv_heads, length, hd), bf16),
                 sds((kv_heads, length, hd), f32), sds((kv_heads, length, hd), f32)],
        flops=10 * heads * rows * length * 128)

    def add_split(keep, recv):
        n, r, c = keep.shape

        def add_split_kernel(ids_ref, keep_r, recv_r, mine, others):
            for d in range(n):
                total = keep_r[d] + decode(recv_r.at[d], r, c)
                if d == 0:
                    mine[...] = total
                else:
                    encode_to(others[d - 1], total)

        return call(add_split_kernel, ids, [keep, recv], [sds((r, c), f32), [coded(r, c)] * (n - 1)])

    kv_first, kv_rest = add_split(kv_keep, swap(kv_give))
    kv_recv = [kv_first] + [send_z(kv_rest[d - 1], d) for d in range(1, nz)]

    def split_rows(g, keep, give, ids_ref):
        k, z0, f0 = ids_ref[0], ids_ref[1], ids_ref[2]

        def one(d, carry):
            for is_keep, side in ((True, k), (False, 1 - k)):
                v = []
                for e in range(nz):
                    at = ((z0 ^ e) * 2 + side) * blk + (f0 ^ d) * dr
                    v.append(g[pl.ds(pl.multiple_of(at, 8), dr), :])
                v = jnp.concatenate(v, axis=0)
                if is_keep:
                    keep[d] = v
                else:
                    encode_to(give, v, d)
            return carry

        lax.fori_loop(0, nf, one, 0)

    def outer_kernel(ids_ref, left, right, keep, give, g):
        g[...] = nn(left[...], right[...])
        split_rows(g, keep, give, ids_ref)

    zr = nz * dr

    def outer(left, right):
        n = right.shape[1]
        return call(outer_kernel, ids, [left, right], [sds((nf, zr, n), f32), stacked(nf, zr, n)],
                    scratch=[sds((width, n), f32)], flops=2 * width * rows * n)

    def over_fsdp(mine, others):
        c = mine.shape[1]
        recv = [send_f(others[d - 1], d) for d in range(1, nf)]

        def over_kernel(ids_ref, mine_r, recv_r, first, rest):
            total = mine_r[...]
            for r in recv_r:
                total = total + decode(r, zr, c)
            first[...] = total[:dr]
            for e in range(1, nz):
                encode_to(rest[e - 1], total[e * dr:(e + 1) * dr])

        first, rest = call(over_kernel, ids, [mine, recv], [sds((dr, c), f32), [coded(dr, c)] * (nz - 1)])
        return first, [send_z(rest[d - 1], d) for d in range(1, nz)]

    out_keep, out_give = outer(attn_t, mgb)
    out_recv = swap(out_give)
    q_keep, q_give = outer(nb_t, dq)
    q_recv = swap(q_give)

    def both_split_kernel(ids_ref, qk, qr, ok, okr, mine, others):
        for d in range(nf):
            total = jnp.concatenate(
                [qk[d] + decode(qr.at[d], zr, qd), ok[d] + decode(okr.at[d], zr, width)], axis=1)
            if d == 0:
                mine[...] = total
            else:
                encode_to(others[d - 1], total)

    both_mine, both_others = call(
        both_split_kernel, ids, [q_keep, q_recv, out_keep, out_recv],
        [sds((zr, qd + width), f32), [coded(zr, qd + width)] * (nf - 1)])
    both_first, both_last = over_fsdp(both_mine, both_others)

    def both_kernel(ids_ref, mine, recv, q_out, o_out):
        t = mine[...]
        for r in recv:
            t = t + decode(r, dr, qd + width)
        q_out[...] = t[:, :qd]
        o_out[...] = t[:, qd:]

    w_query_grad, w_out_grad = call(
        both_kernel, ids, [both_first, both_last], [sds((dr, qd), f32), sds((dr, width), f32)])

    def last_kernel(ids_ref, kvp, dqr, x, nbt, gain, fgr, mgr, own, oth, cos, sin, grad_out, keep, give, w, g):
        assemble(w, own, oth, ids_ref)
        kv = kvp[0][...]
        for i in range(1, nz):
            kv = kv + decode(kvp[i], rows, 2 * kvd)
        c = cos[...]
        s = sin[...]
        turn = jnp.transpose(kv[:, :kvd])
        pieces = []
        for h in range(kv_heads):
            a = turn[h * hd:h * hd + half]
            d = turn[h * hd + half:(h + 1) * hd]
            pieces += [a * c + d * s, d * c - a * s]
        dkb = jnp.transpose(jnp.concatenate(pieces, axis=0)).astype(bf16)
        dvb = kv[:, kvd:].astype(bf16)
        pg = jnp.concatenate([dqr[...], dkb, dvb], axis=1)
        ing = nt(pg, w[:, :qkv])
        xf = x[...].astype(f32)
        scale = lax.rsqrt(jnp.mean(xf * xf, axis=-1, keepdims=True) + epsilon)
        plain = xf * scale
        ag = jnp.sum(ing * plain, axis=0, keepdims=True)
        e = ing * gain[0:1]
        grad_out[...] = mgr[...] + scale * (e - plain * jnp.mean(e * plain, axis=-1, keepdims=True))
        g[:, :2 * kvd] = nn(nbt[...], pg[:, qd:])
        sub = lax.broadcasted_iota(jnp.int32, (128, width), 0)
        both = jnp.where(sub == 0, ag, jnp.where(sub == 1, fgr[0:1], 0.0))
        g[:, 2 * kvd:] = jnp.transpose(both)
        split_rows(g, keep, give, ids_ref)

    sc = 2 * kvd + 128
    input_grad, keep, give = call(
        last_kernel, ids, [kv_recv, dq, x_in, nb_t, gains, fg, mid_grad, attn_own, attn_oth, cos_t, sin_t],
        [sds((rows, width), f32), sds((nf, zr, sc), f32), stacked(nf, zr, sc)],
        scratch=[sds((width, cols), bf16), sds((width, sc), f32)],
        flops=2 * rows * width * (qkv + 2 * kvd))
    mine, others = add_split(keep, swap(give))
    rest_first, rest_last = over_fsdp(mine, others)

    def row(col):
        a = lax.broadcasted_iota(jnp.int32, (dr, dr), 0)
        b = lax.broadcasted_iota(jnp.int32, (dr, dr), 1)
        return jnp.sum(jnp.where(a == b, jnp.broadcast_to(col, (dr, dr)), 0.0), axis=0, keepdims=True)

    def rest_kernel(ids_ref, mine_r, recv, k_out, v_out, a_out, f_out):
        t = mine_r[...]
        for r in recv:
            t = t + decode(r, dr, sc)
        k_out[...] = t[:, :kvd]
        v_out[...] = t[:, kvd:2 * kvd]
        a_out[...] = row(t[:, 2 * kvd:2 * kvd + 1])
        f_out[...] = row(t[:, 2 * kvd + 1:2 * kvd + 2])

    w_key_grad, w_value_grad, gain_a_grad, gain_f_grad = call(
        rest_kernel, ids, [rest_first, rest_last],
        [sds((dr, kvd), f32), sds((dr, kvd), f32), sds((1, dr), f32), sds((1, dr), f32)])

    in_parts = []
    for keep, give in in_pairs:
        mine, others = add_split(keep, swap(give))
        in_parts.append((mine, [send_z(others[d - 1], d) for d in range(1, nz)]))

    def in_split_kernel(ids_ref, mines, recvs, outs, down, s):
        for ch, base, mine, recv in zip(chunks, bases, mines, recvs):
            t = mine[...]
            for r in recv:
                t = t + decode(r, blk + ch.rows, ch.wide)
            s[:, base:base + ch.wide] = t[:blk]
            down[ch.off:ch.off + ch.fr, :] = ch.unfold(t[blk:], width)
        for d in range(nf):
            v = s[pl.ds(pl.multiple_of((ids_ref[2] ^ d) * dr, 8), dr), :]
            if d == 0:
                outs[0][...] = v
            else:
                encode_to(outs[d], v)

    in_rows, w_down_grad = call(
        in_split_kernel, ids, [[p[0] for p in in_parts], [p[1] for p in in_parts]],
        [[sds((dr, wide_all), f32)] + [coded(dr, wide_all)] * (nf - 1), sds((fr, width), f32)],
        scratch=[sds((blk, wide_all), f32)])
    in_pieces = [in_rows[0]] + [send_f(in_rows[d], d) for d in range(1, nf)]

    def unpack_kernel(ids_ref, p, g_out, u_out, s):
        for d in range(nf):
            s[ids_ref[2] ^ d] = p[d][...] if d == 0 else decode(p[d], dr, wide_all)
        for w, j, at, to, n in columns(g_out, u_out):
            w[:, at:at + n] = s[j, :, to:to + n]

    w_gate_grad, w_up_grad = call(
        unpack_kernel, ids, [in_pieces], [sds(w_gate.shape, f32), sds(w_up.shape, f32)],
        scratch=[sds((nf, dr, wide_all), f32)])

    return (
        block_out[None],
        input_grad[None],
        gain_a_grad[0],
        w_query_grad,
        w_key_grad,
        w_value_grad,
        w_out_grad,
        gain_f_grad[0],
        w_gate_grad,
        w_up_grad,
        w_down_grad,
    )


def make_body(nc, nf):
    general = general_body(nc, nf)

    def body(*args):
        rows = args[0].shape[1]
        if tiled_fits(nc, nf, args[3].shape[0], args[10].shape[0], rows, args[4].shape[1], args[0].shape[2]):
            return tiled_body(nc, nf, args)
        return general(*args)

    return body


def solution(mesh):
    tokens = P("fsdp", "ctx", None)
    shard = P(("ctx", "fsdp"))
    shard2 = P(("ctx", "fsdp"), None)
    return jax.shard_map(
        make_body(mesh.shape["ctx"], mesh.shape["fsdp"]),
        mesh=mesh,
        in_specs=(tokens, P("fsdp", "ctx"), shard, shard2, shard2, shard2, shard2, shard,
                  shard2, shard2, shard2, tokens),
        out_specs=(tokens, tokens, shard, shard2, shard2, shard2, shard2, shard,
                   shard2, shard2, shard2),
        check_vma=False,
    )
```
